32 devices in a mesh: cls: 8 (over z, x), img: 4 (over y, core).
Axes of the slice: x: 2, y: 2, z: 4, core: 2. Of those that a mesh axis runs over, the one named last changes fastest.
Arguments:
- images: bfloat16 [512, 9216], P(('cls', 'img')), may hold values from -9 to 9
- ctf: bfloat16 [512, 4608], P(('cls', 'img')), may hold values from -1 to 1
- classes: int32 [512, 4], P(('cls', 'img')), may hold values from 0 to 55, as said below
- class_place: int32 [56], replicated, may hold values from 0 to 55, as said below
- references: bfloat16 [56, 9216], P('cls'), may hold values from -3 to 3
- sigma2: float32 [64], replicated, may hold values from 0.05 to 4, as said below
Outputs:
- new_references: float32 [56, 9216], P('cls', 'img')
The draws below stay inside these ranges and needn't reach their ends.
Inputs may be any that keep to these rules, and one draw needn't show every extreme that they name: Each particle names 4 different classes whose table rows class_place[k] lie in 4 different groups of 7 consecutive table rows. Among the 16 particles of one device (aligned blocks of 16 rows) at most 8 list entries fall in one group, and in every block some group receives exactly 8. A permutation: class k is held in table row class_place[k]. `sigma2`: positive noise powers.
All inputs are finite; a program needn't handle non-finite values.
Results may differ from the reference program's by a relative error of at most 0.0018.
Values may be sent and summed in bfloat16 or wider, within the bound.
A program may use at most 128 MiB of HBM per device.

```python
import math
import jax
import jax.numpy as jnp
from jax import lax

S = 64
NA = 72
TOP = 4
K_DEV = 7
P_DEV = 16
CAP = 8
K = 56
NP = 512


def routing_tables(key):
    owners = K // K_DEV
    blocks = NP // P_DEV
    groups = blocks // owners
    pick_count = TOP * P_DEV
    placement = jax.random.permutation(jax.random.fold_in(key, 7), K).astype(jnp.int32)
    inverse = jnp.zeros((K,), jnp.int32).at[placement].set(jnp.arange(K, dtype=jnp.int32))
    hot_group = jax.random.randint(jax.random.fold_in(key, 8), (groups,), 0, owners)
    hot_block = hot_group[jnp.arange(blocks) % groups]
    block_keys = jax.random.split(jax.random.fold_in(key, 9), blocks)
    remaining = pick_count - CAP
    even_load = remaining // (owners - 1)
    extra_load = remaining % (owners - 1)
    pair_count = max((owners - 1) // 2, 1)

    def one_block(block_key, hot_owner):
        key_rank, key_move, key_order, key_offset, key_rows = jax.random.split(block_key, 5)
        ordering = jax.random.permutation(key_rank, owners)
        ranking = jnp.zeros((owners,), jnp.int32).at[ordering].set(jnp.arange(owners, dtype=jnp.int32))
        other_rank = ranking - (ranking > ranking[hot_owner]).astype(jnp.int32)
        loads = even_load + (other_rank < extra_load).astype(jnp.int32)
        pair_index = jnp.arange(pair_count, dtype=jnp.int32)
        low_load = even_load + (2 * pair_index < extra_load).astype(jnp.int32)
        high_load = even_load + (2 * pair_index + 1 < extra_load).astype(jnp.int32)
        move_limit = jnp.maximum(jnp.minimum(low_load, CAP - high_load), 0)
        shifted_by = jax.random.randint(key_move, (pair_count,), 0, move_limit + 1)
        paired = other_rank < 2 * ((owners - 1) // 2)
        partner = jnp.minimum(other_rank // 2, pair_count - 1)
        change = jnp.where(other_rank % 2 == 0, -shifted_by[partner], shifted_by[partner])
        loads = jnp.where(paired, loads + change, loads)
        loads = jnp.where(jnp.arange(owners) == hot_owner, CAP, loads).astype(jnp.int32)
        sequence = jax.random.permutation(key_order, owners)
        ordered = loads[sequence]
        run_end = jnp.cumsum(ordered)
        starts = run_end - ordered
        pick_slot = jnp.arange(pick_count, dtype=jnp.int32)
        position = jnp.sum((pick_slot[:, None] >= run_end[None, :]).astype(jnp.int32), axis=1)
        owner_id = sequence[position]
        within = pick_slot - starts[position]
        offset = jax.random.randint(key_offset, (owners,), 0, K_DEV)
        table_row = owner_id * K_DEV + (offset[owner_id] + within) % K_DEV
        chosen = inverse[table_row].reshape(TOP, P_DEV).T
        return chosen[jax.random.permutation(key_rows, P_DEV)]
    class_lists = jax.vmap(one_block)(block_keys, hot_block)
    return (placement, class_lists.reshape(NP, TOP).astype(jnp.int32))


def bright_setup(key):
    bright_count = max(1, K // 32)
    bright_rows = jax.random.permutation(jax.random.fold_in(key, 21), K)[:bright_count]
    is_bright = jnp.zeros((K,), jnp.bool_).at[bright_rows].set(True)
    strength = jax.random.uniform(jax.random.fold_in(key, 22), (K,), jnp.float32, 1.5, 3.0)
    amplitude = jnp.where(is_bright, jnp.sqrt(536.0 * strength / (S * NA)), 0.05)
    return (is_bright, amplitude)


def draw_classes(key, part):
    return routing_tables(key)[1]


def draw_class_place(key, part):
    return routing_tables(key)[0]


def draw_sigma2(key, part):
    spread = jax.random.uniform(key, (S,), jnp.float32, math.log(0.5), math.log(4.0))
    noise_power = jnp.exp(spread)
    return noise_power.astype(jnp.float32)


def draw_references(key, part):
    is_bright, amplitude = bright_setup(key)
    inner = jax.random.fold_in(key, 23)
    base = jax.random.truncated_normal(inner, -3.0, 3.0, (K, S * 2 * NA), jnp.float32)
    return (base * amplitude[:, None]).astype(jnp.bfloat16)


def draw_ctf(key, part):
    return jax.random.uniform(jax.random.fold_in(key, 24), (NP, S * NA), jnp.float32, -1.0, 1.0).astype(jnp.bfloat16)


def draw_images(key, part):
    placement, class_lists = routing_tables(key)
    is_bright, amplitude = bright_setup(key)
    inner = jax.random.fold_in(key, 25)
    noise = jax.random.truncated_normal(inner, -6.0, 6.0, (NP, S, 2, NA), jnp.float32)
    rows = placement[class_lists]
    hit = is_bright[rows]
    has_bright = jnp.any(hit, axis=1)
    first = jnp.argmax(hit.astype(jnp.int32), axis=1)
    row_pick = jnp.take_along_axis(rows, first[:, None], axis=1)[:, 0]
    table = draw_references(key, part).reshape(K, S, 2, NA)
    picked = table[row_pick]
    turn_by = jax.random.randint(jax.random.fold_in(key, 26), (NP,), 0, NA)
    index = (jnp.arange(NA, dtype=jnp.int32)[None, :] - turn_by[:, None]) % NA
    turned = jnp.take_along_axis(picked, index[:, None, None, :], axis=3)
    ctf_values = draw_ctf(key, part).reshape(NP, S, NA)
    aligned = ctf_values[:, :, None, :] * turned
    images = noise + jnp.where(has_bright[:, None, None, None], aligned, 0.0)
    return images.reshape(NP, S * 2 * NA).astype(jnp.bfloat16)


def setup_inputs(seed: int = 0) -> dict:
    streams_of = jax.random.split(jax.random.key(seed), 7)
    return {
        "images": draw_images(jax.random.fold_in(streams_of[6], 71), 0),
        "ctf": draw_ctf(jax.random.fold_in(streams_of[6], 71), 0),
        "classes": draw_classes(jax.random.fold_in(streams_of[6], 71), 0),
        "class_place": draw_class_place(jax.random.fold_in(streams_of[6], 71), 0),
        "references": draw_references(jax.random.fold_in(streams_of[6], 71), 0),
        "sigma2": draw_sigma2(jax.random.fold_in(streams_of[6], 71), 0),
    }


def reference(images, ctf, classes, class_place, references, sigma2):
    shells = sigma2.shape[0]
    angles = ctf.shape[1] // shells
    class_total = class_place.shape[0]
    ref_table = references.astype(jnp.float32).reshape(class_total, shells, 2, angles)
    ref_power = jnp.sum(ref_table * ref_table, axis=2).astype(jnp.bfloat16)
    ref_power = lax.optimization_barrier(ref_power).astype(jnp.float32)
    table_hat = jnp.fft.rfft(ref_table, axis=-1)
    power_hat = jnp.fft.rfft(ref_power, axis=-1)
    table_rows = class_place[classes].astype(jnp.int32)
    inverse_sigma = 1.0 / sigma2
    block_count = 32
    block_rows = images.shape[0] // block_count
    num_zero = jnp.zeros(table_hat.shape, table_hat.dtype)
    den_zero = jnp.zeros(power_hat.shape, power_hat.dtype)

    def advance(carry, block_data):
        num_hat, den_hat = carry
        image_block, ctf_block, rows_block = block_data
        scaling = ctf_block.astype(jnp.float32).reshape(block_rows, shells, angles) * inverse_sigma[None, :, None]
        weighted = (image_block.astype(jnp.float32).reshape(block_rows, shells, 2, angles) * scaling[:, :, None, :]).astype(jnp.bfloat16)
        ctf_power = (ctf_block.astype(jnp.float32).reshape(block_rows, shells, angles) * scaling).astype(jnp.bfloat16)
        weighted, ctf_power = lax.optimization_barrier((weighted, ctf_power))
        weighted_hat = jnp.fft.rfft(weighted.astype(jnp.float32), axis=-1)
        ctf_hat = jnp.fft.rfft(ctf_power.astype(jnp.float32), axis=-1)
        ref_rows = table_hat[rows_block]
        pow_rows = power_hat[rows_block]
        cross_term = jnp.fft.irfft(jnp.sum(weighted_hat[:, None] * jnp.conj(ref_rows), axis=(2, 3)), n=angles, axis=-1)
        quad_term = jnp.fft.irfft(jnp.sum(ctf_hat[:, None] * jnp.conj(pow_rows), axis=2), n=angles, axis=-1)
        logits = cross_term - 0.5 * quad_term
        highest = jnp.max(logits, axis=(1, 2), keepdims=True)
        exponent = jnp.exp(logits - highest)
        posterior = (exponent / jnp.sum(exponent, axis=(1, 2), keepdims=True)).astype(jnp.bfloat16)
        posterior = lax.optimization_barrier(posterior).astype(jnp.float32)
        post_hat = jnp.conj(jnp.fft.rfft(posterior, axis=-1))
        num_hat = num_hat.at[rows_block].add(weighted_hat[:, None] * post_hat[:, :, None, None, :])
        den_hat = den_hat.at[rows_block].add(ctf_hat[:, None] * post_hat[:, :, None, :])
        return (num_hat, den_hat), None

    block_data = (images.reshape(block_count, block_rows, -1), ctf.reshape(block_count, block_rows, -1), table_rows.reshape(block_count, block_rows, -1))
    (num_hat, den_hat), unused = lax.scan(advance, (num_zero, den_zero), block_data)
    numerator = jnp.fft.irfft(num_hat, n=angles, axis=-1)
    denominator = jnp.fft.irfft(den_hat, n=angles, axis=-1)
    updated = numerator / (denominator[:, :, None, :] + 1.0)
    return updated.reshape(class_total, -1)
```

```python
import functools

import jax
import jax.numpy as jnp
from jax import lax
from jax.experimental import pallas as pl
from jax.experimental.pallas import tpu as pltpu
from jax.sharding import PartitionSpec as P

MESH = pl.DeviceIdType.MESH
VMEM = pltpu.VMEM
F32 = jnp.float32
BF16 = jnp.bfloat16
LANES = 128


def vmem_specs(count):
    return [pl.BlockSpec(memory_space=pltpu.VMEM)] * count


def greet(groups):
    barrier = pltpu.get_barrier_semaphore()
    total = 0
    for axis, size in groups:
        me = lax.axis_index(axis)
        for step in range(1, size):
            peer = lax.rem(me + step, size)
            pl.semaphore_signal(barrier, inc=1, device_id={axis: peer}, device_id_type=MESH)
            total += 1
    pl.semaphore_wait(barrier, total)


def spread_kernel(owners, fellows, w_ref, r_ref, t_ref, wall, rall, tall, own_sem, ws, wr, rs, rr, ts, tr):
    my_owner = lax.axis_index("cls")
    my_fellow = lax.axis_index("img")
    greet((("cls", owners), ("img", fellows)))
    copies = []
    for step in range(1, owners):
        peer = lax.rem(my_owner + step, owners)
        copies.append(
            pltpu.make_async_remote_copy(
                src_ref=r_ref,
                dst_ref=rall.at[my_owner],
                send_sem=rs.at[step],
                recv_sem=rr.at[step],
                device_id={"cls": peer},
                device_id_type=MESH,
            )
        )
    for step in range(1, fellows):
        peer = lax.rem(my_fellow + step, fellows)
        copies.append(
            pltpu.make_async_remote_copy(
                src_ref=t_ref,
                dst_ref=tall.at[my_fellow],
                send_sem=ts.at[step],
                recv_sem=tr.at[step],
                device_id={"img": peer},
                device_id_type=MESH,
            )
        )
        copies.append(
            pltpu.make_async_remote_copy(
                src_ref=w_ref.at[peer],
                dst_ref=wall.at[my_fellow],
                send_sem=ws.at[step],
                recv_sem=wr.at[step],
                device_id={"img": peer},
                device_id_type=MESH,
            )
        )
    for copy in copies:
        copy.start()
    own = [
        pltpu.make_async_copy(w_ref.at[my_fellow], wall.at[my_fellow], own_sem.at[0]),
        pltpu.make_async_copy(r_ref, rall.at[my_owner], own_sem.at[1]),
        pltpu.make_async_copy(t_ref, tall.at[my_fellow], own_sem.at[2]),
    ]
    for copy in own:
        copy.start()
    for copy in own:
        copy.wait()
    for copy in copies:
        copy.wait()


def exchange_kernel(axis, size, x_ref, out_ref, own_sem, send, recv, *, split):
    me = lax.axis_index(axis)
    greet(((axis, size),))
    copies = []
    for step in range(1, size):
        peer = lax.rem(me + step, size)
        copies.append(
            pltpu.make_async_remote_copy(
                src_ref=x_ref.at[peer] if split else x_ref,
                dst_ref=out_ref.at[me],
                send_sem=send.at[step],
                recv_sem=recv.at[step],
                device_id={axis: peer},
                device_id_type=MESH,
            )
        )
    for copy in copies:
        copy.start()
    own = pltpu.make_async_copy(x_ref.at[me] if split else x_ref, out_ref.at[me], own_sem.at[0])
    own.start()
    own.wait()
    for copy in copies:
        copy.wait()


def exchange(x, axis, size, split, collective_id):
    block = x.shape[1:] if split else x.shape
    return pl.pallas_call(
        functools.partial(exchange_kernel, axis, size, split=split),
        out_shape=jax.ShapeDtypeStruct((size,) + block, x.dtype),
        in_specs=vmem_specs(1),
        out_specs=pl.BlockSpec(memory_space=pltpu.VMEM),
        scratch_shapes=[
            pltpu.SemaphoreType.DMA((1,)),
            pltpu.SemaphoreType.DMA((size,)),
            pltpu.SemaphoreType.DMA((size,)),
        ],
        compiler_params=pltpu.CompilerParams(collective_id=collective_id, has_side_effects=True),
    )(x)


def lane_of(shape):
    return lax.broadcasted_iota(jnp.int32, shape, len(shape) - 1)


def roll(x, shift):
    return pltpu.roll(x, shift % LANES, x.ndim - 1)


def score_kernel(dims, rows_ref, wall, rall, logits_ref, weights_ref, table, low, high):
    fellows, particles, owners, slots, top, angles, half = dims
    width = 2 * half
    per_pack = LANES // width
    per_den = LANES // half
    tall_rows = table.shape[1]
    num_packs = particles // per_pack
    lane = lane_of((angles, LANES))
    zero_tail = jnp.zeros((LANES - angles, LANES), F32)

    def place(fellow, carry):
        for i in range(particles):
            num = wall[fellow, i // per_pack].astype(F32)
            den = wall[fellow, num_packs + i // per_den].astype(F32)
            num = roll(num, -width * (i % per_pack))
            den = roll(den, width - half * (i % per_den))
            joined = jnp.where(lane < width, num, jnp.where(lane < width + half, den, 0.0))
            weights_ref[fellow * particles + i] = jnp.concatenate([joined, zero_tail], axis=0).astype(BF16)
        return carry

    lax.fori_loop(0, fellows, place, 0)

    def tabulate(owner, carry):
        for t in range(slots):
            ref = roll(rall[owner, t // per_pack].astype(F32), -width * (t % per_pack))
            square = ref * ref
            power = (square + roll(square, -half)).astype(BF16).astype(F32) * -0.5
            power = roll(power, width)
            joined = jnp.where(lane < width, ref, jnp.where(lane < width + half, power, 0.0))
            table[owner * slots + t] = jnp.concatenate(
                [joined, jnp.zeros((tall_rows - angles, LANES), F32)], axis=0
            ).astype(BF16)
        return carry

    lax.fori_loop(0, owners, tabulate, 0)
    cut = (angles // 16) * 8 + (8 if (angles // 8) % 2 else 0)
    tiles = angles // 8

    def pair(m, carry):
        lows = []
        highs = []
        for k in range(2):
            i = 2 * m + k
            refs = jnp.concatenate([table[rows_ref[i, j]] for j in range(top)], axis=0)
            grid = lax.dot_general(
                refs, weights_ref[i], (((1,), (1,)), ((), ())), preferred_element_type=F32
            )
            for j in range(top):
                base = j * tall_rows
                lo = grid[base : base + 8]
                for tile in range(1, cut // 8):
                    lo = lo + roll(grid[base + 8 * tile : base + 8 * tile + 8], 8 * tile)
                hi = grid[base + cut : base + cut + 8]
                for tile in range(cut // 8 + 1, tiles):
                    hi = hi + roll(grid[base + 8 * tile : base + 8 * tile + 8], 8 * tile - cut)
                lo = pltpu.roll(lo, 0, 1, stride=1, stride_axis=0)
                hi = pltpu.roll(hi, 0, 1, stride=1, stride_axis=0)
                lows.append(jnp.sum(lo, axis=0, keepdims=True))
                highs.append(jnp.sum(hi, axis=0, keepdims=True))
        low[m] = jnp.concatenate(lows, axis=0)
        high[m] = jnp.concatenate(highs, axis=0)
        return carry

    lax.fori_loop(0, low.shape[0], pair, 0)
    lo = low[...].reshape(-1, LANES)
    hi = high[...].reshape(-1, LANES)
    spot = lane_of(lo.shape)
    total = roll(lo, 1) + jnp.where(spot < cut, roll(lo, 1 - angles), 0.0)
    back = angles - 1 - cut
    total = total + roll(hi, -back) + jnp.where(spot >= cut + 1, roll(hi, cut + 1), 0.0)
    logits_ref[...] = jnp.where(spot < angles, total, 0.0)


def group_of(x, top, combine):
    row = lax.broadcasted_iota(jnp.int32, x.shape, 0)
    count = x.shape[0]
    step = 1
    while step < top:
        swapped = jnp.where(
            (row // step) % 2 == 0, pltpu.roll(x, count - step, 0), pltpu.roll(x, step, 0)
        )
        x = combine(x, swapped)
        step *= 2
    return x


def total_kernel(dims, rows_ref, parts, weights_ref, out_ref, acc, ext_lo, ext_hi):
    fellows, particles, owners, slots, top, angles, half = dims
    width = 2 * half
    per_pack = LANES // width
    per_den = LANES // half
    num_packs = slots // per_pack
    cut = (angles // 16) * 8 + (8 if (angles // 8) % 2 else 0)
    tiles = angles // 8
    tall_rows = -(-angles // 16) * 16
    logits = parts[0]
    for fellow in range(1, fellows):
        logits = logits + parts[fellow]
    spot = lane_of(logits.shape)
    inside = spot < angles
    highest = jnp.max(jnp.where(inside, logits, -jnp.inf), axis=1, keepdims=True)
    highest = group_of(jnp.broadcast_to(highest, logits.shape), top, jnp.maximum)
    exponent = jnp.where(inside, jnp.exp(logits - highest), 0.0)
    summed = jnp.sum(exponent, axis=1, keepdims=True)
    summed = group_of(jnp.broadcast_to(summed, logits.shape), top, jnp.add)
    post = (exponent / summed).astype(BF16).astype(F32)
    lo = jnp.where(inside, post, roll(post, LANES - angles))
    hi = jnp.where((spot >= cut) & inside, roll(post, cut), roll(post, cut - angles))
    ext_lo[...] = lo.reshape(ext_lo.shape)
    ext_hi[...] = hi.reshape(ext_hi.shape)
    acc[...] = jnp.zeros_like(acc)

    def pair(m, carry):
        lo_rows = ext_lo[m]
        hi_rows = ext_hi[m]
        for k in range(2):
            i = 2 * m + k
            turned = []
            for j in range(top):
                e = k * top + j
                first = pltpu.roll(
                    jnp.broadcast_to(lo_rows[e : e + 1], (8, LANES)), 0, 1, stride=1, stride_axis=0
                )
                second = pltpu.roll(
                    jnp.broadcast_to(hi_rows[e : e + 1], (8, LANES)), 0, 1, stride=1, stride_axis=0
                )
                for tile in range(tiles):
                    if 8 * tile < cut:
                        turned.append(roll(first, 8 * tile) if tile else first)
                    else:
                        shift = 8 * tile - cut
                        turned.append(roll(second, shift) if shift else second)
                for tile in range(tiles, tall_rows // 8):
                    turned.append(second)
            circle = jnp.concatenate(turned, axis=0).astype(BF16)
            grid = jnp.dot(circle, weights_ref[i], preferred_element_type=F32)
            for j in range(top):
                row = rows_ref[i, j]
                acc[row] = acc[row] + grid[j * tall_rows : j * tall_rows + angles]
        return carry

    lax.fori_loop(0, ext_lo.shape[0], pair, 0)
    lane = lane_of((angles, LANES))

    def pack(owner, carry):
        nums = [None] * num_packs
        dens = [None] * (slots // per_den)
        for t in range(slots):
            value = acc[owner * slots + t]
            g, u = t % per_pack, t // per_pack
            num = roll(value, width * g)
            nums[u] = num if g == 0 else jnp.where(lane >= width * g, num, nums[u])
            h, v = t % per_den, t // per_den
            den = roll(value, half * h - width)
            dens[v] = den if h == 0 else jnp.where(lane >= half * h, den, dens[v])
        for u, value in enumerate(nums + dens):
            out_ref[owner, u] = value.astype(BF16)
        return carry

    lax.fori_loop(0, owners, pack, 0)


def gather_kernel(axis, size, x_ref, out_ref, landed, send, recv):
    me = lax.axis_index(axis)
    greet(((axis, size),))
    copies = []
    for step in range(1, size):
        peer = lax.rem(me + step, size)
        copies.append(
            pltpu.make_async_remote_copy(
                src_ref=x_ref.at[peer],
                dst_ref=landed.at[step - 1],
                send_sem=send.at[step],
                recv_sem=recv.at[step],
                device_id={axis: peer},
                device_id_type=MESH,
            )
        )
    for copy in copies:
        copy.start()
    total = x_ref[me].astype(F32)
    for step in range(1, size):
        copies[step - 1].wait_recv()
        total = total + landed[step - 1].astype(F32)
    out_ref[...] = total
    for copy in copies:
        copy.wait_send()


def on_device(images, ctf, classes, class_place, references, sigma2):
    shells = sigma2.shape[0]
    angles = ctf.shape[1] // shells
    particles = images.shape[0]
    per_owner = references.shape[0]
    top = classes.shape[1]
    owners = lax.axis_size("cls")
    fellows = lax.axis_size("img")
    my_fellow = lax.axis_index("img")
    half = shells // fellows
    width = 2 * half
    per_pack = LANES // width
    per_den = LANES // half
    slots = -(-per_owner // per_den) * per_den
    dims = (fellows, particles, owners, slots, top, angles, half)

    scaling = ctf.astype(F32).reshape(particles, shells, angles) * (1.0 / sigma2)[None, :, None]
    weighted = (
        images.astype(F32).reshape(particles, shells, 2, angles) * scaling[:, :, None, :]
    ).astype(BF16)
    ctf_power = (ctf.astype(F32).reshape(particles, shells, angles) * scaling).astype(BF16)
    num = weighted.reshape(particles // per_pack, per_pack, fellows, half, 2, angles)
    num = num.transpose(2, 0, 5, 1, 4, 3).reshape(fellows, -1, angles, LANES)
    den = ctf_power.reshape(particles // per_den, per_den, fellows, half, angles)
    den = den.transpose(2, 0, 4, 1, 3).reshape(fellows, -1, angles, LANES)
    send = jnp.concatenate([num, den], axis=1)
    mine = lax.dynamic_slice_in_dim(references, my_fellow * (width * angles), width * angles, 1)
    mine = jnp.pad(mine, ((0, slots - per_owner), (0, 0)))
    mine = mine.reshape(slots // per_pack, per_pack, half, 2, angles)[..., ::-1]
    mine = mine.transpose(0, 4, 1, 3, 2).reshape(-1, angles, LANES)

    lookup = classes[:, :, None] == jnp.arange(class_place.shape[0], dtype=jnp.int32)[None, None, :]
    table_rows = jnp.sum(jnp.where(lookup, class_place[None, None, :], 0), axis=2)
    rows = (table_rows // per_owner) * slots + table_rows % per_owner
    rows = jnp.pad(rows, ((0, 0), (0, LANES - top)))

    packs = send.shape[1]
    wall, rall, tall = pl.pallas_call(
        functools.partial(spread_kernel, owners, fellows),
        out_shape=(
            jax.ShapeDtypeStruct((fellows, packs, angles, LANES), BF16),
            jax.ShapeDtypeStruct((owners,) + mine.shape, BF16),
            jax.ShapeDtypeStruct((fellows, particles, LANES), jnp.int32),
        ),
        in_specs=vmem_specs(3),
        out_specs=tuple(vmem_specs(3)),
        scratch_shapes=[
            pltpu.SemaphoreType.DMA((3,)),
            pltpu.SemaphoreType.DMA((fellows,)),
            pltpu.SemaphoreType.DMA((fellows,)),
            pltpu.SemaphoreType.DMA((owners,)),
            pltpu.SemaphoreType.DMA((owners,)),
            pltpu.SemaphoreType.DMA((fellows,)),
            pltpu.SemaphoreType.DMA((fellows,)),
        ],
        compiler_params=pltpu.CompilerParams(collective_id=0, has_side_effects=True),
    )(send, mine, rows)
    everyone = fellows * particles
    row_list = tall[:, :, :top].reshape(everyone, top)
    tall_rows = -(-angles // 16) * 16
    pairs = everyone // 2
    smem = pl.BlockSpec(memory_space=pltpu.SMEM)
    logits, weights = pl.pallas_call(
        functools.partial(score_kernel, dims),
        out_shape=(
            jax.ShapeDtypeStruct((everyone * top, LANES), F32),
            jax.ShapeDtypeStruct((everyone, LANES, LANES), BF16),
        ),
        in_specs=[smem] + vmem_specs(2),
        out_specs=tuple(vmem_specs(2)),
        scratch_shapes=[
            VMEM((owners * slots, tall_rows, LANES), BF16),
            VMEM((pairs, 2 * top, LANES), F32),
            VMEM((pairs, 2 * top, LANES), F32),
        ],
    )(row_list, wall, rall)
    parts = exchange(logits, "img", fellows, False, 1)
    sums = pl.pallas_call(
        functools.partial(total_kernel, dims),
        out_shape=jax.ShapeDtypeStruct(
            (owners, slots // per_pack + slots // per_den, angles, LANES), BF16
        ),
        in_specs=[smem] + vmem_specs(2),
        out_specs=pl.BlockSpec(memory_space=pltpu.VMEM),
        scratch_shapes=[
            VMEM((owners * slots, angles, LANES), F32),
            VMEM((pairs, 2 * top, LANES), F32),
            VMEM((pairs, 2 * top, LANES), F32),
        ],
    )(row_list, parts, weights)
    share = pl.pallas_call(
        functools.partial(gather_kernel, "cls", owners),
        out_shape=jax.ShapeDtypeStruct(sums.shape[1:], F32),
        in_specs=vmem_specs(1),
        out_specs=pl.BlockSpec(memory_space=pltpu.VMEM),
        scratch_shapes=[
            VMEM((owners - 1,) + sums.shape[1:], BF16),
            pltpu.SemaphoreType.DMA((owners,)),
            pltpu.SemaphoreType.DMA((owners,)),
        ],
        compiler_params=pltpu.CompilerParams(collective_id=2, has_side_effects=True),
    )(sums)
    num_packs = slots // per_pack
    num = share[:num_packs].reshape(num_packs, angles, per_pack, 2, half)
    num = num.transpose(0, 2, 4, 3, 1).reshape(slots, half, 2, angles)[:per_owner]
    den = share[num_packs:].reshape(-1, angles, per_den, half)
    den = den.transpose(0, 2, 3, 1).reshape(slots, half, 1, angles)[:per_owner]
    return (num / (den + 1.0)).reshape(per_owner, -1)


def solution(mesh):
    in_specs = (
        P(("cls", "img"), None),
        P(("cls", "img"), None),
        P(("cls", "img"), None),
        P(),
        P("cls", None),
        P(),
    )
    out_specs = P("cls", "img")
    return jax.shard_map(
        on_device, mesh=mesh, in_specs=in_specs, out_specs=out_specs, check_vma=False
    )
```

```python
import functools

import jax
import jax.numpy as jnp
from jax import lax
from jax.experimental import pallas as pl
from jax.experimental.pallas import tpu as pltpu
from jax.sharding import PartitionSpec as P

MESH = pl.DeviceIdType.MESH
VMEM = pltpu.VMEM
F32 = jnp.float32
BF16 = jnp.bfloat16
LANES = 128


def vmem_specs(count):
    return [pl.BlockSpec(memory_space=pltpu.VMEM)] * count


def greet(groups):
    barrier = pltpu.get_barrier_semaphore()
    total = 0
    for axis, size in groups:
        me = lax.axis_index(axis)
        for step in range(1, size):
            peer = lax.rem(me + step, size)
            pl.semaphore_signal(barrier, inc=1, device_id={axis: peer}, device_id_type=MESH)
            total += 1
    pl.semaphore_wait(barrier, total)


def lane_of(shape):
    return lax.broadcasted_iota(jnp.int32, shape, len(shape) - 1)


def roll(x, shift):
    return pltpu.roll(x, shift % LANES, x.ndim - 1)


def score_kernel(
    dims, w_ref, r_ref, t_ref, parts, weights_ref, tall, wall, rall, rows_ref, table, low, high,
    own_sem, ws, wr, rs, rr, ts, tr, ls, lr,
):
    fellows, particles, owners, slots, top, angles, half = dims
    width = 2 * half
    per_pack = LANES // width
    per_den = LANES // half
    tall_rows = table.shape[1]
    num_packs = particles // per_pack
    tiles = angles // 8
    cut = (tiles // 2 + tiles % 2) * 8
    my_owner = lax.axis_index("cls")
    my_fellow = lax.axis_index("img")
    greet((("cls", owners), ("img", fellows)))

    def remote(src, dst, send, recv, axis, peer):
        return pltpu.make_async_remote_copy(
            src_ref=src,
            dst_ref=dst,
            send_sem=send,
            recv_sem=recv,
            device_id={axis: peer},
            device_id_type=MESH,
        )

    row_copies = []
    ref_copies = []
    image_copies = []
    for step in range(1, fellows):
        peer = lax.rem(my_fellow + step, fellows)
        row_copies.append(remote(t_ref, tall.at[my_fellow], ts.at[step], tr.at[step], "img", peer))
        image_copies.append(
            remote(w_ref.at[peer], wall.at[my_fellow], ws.at[step], wr.at[step], "img", peer)
        )
    for step in range(1, owners):
        peer = lax.rem(my_owner + step, owners)
        ref_copies.append(remote(r_ref, rall.at[my_owner], rs.at[step], rr.at[step], "cls", peer))
    for copy in row_copies + ref_copies + image_copies:
        copy.start()
    own_rows = pltpu.make_async_copy(t_ref, tall.at[my_fellow], own_sem.at[0])
    own_rows.start()

    lane = lane_of((angles, LANES))
    zero_tail = jnp.zeros((LANES - angles, LANES), F32)

    def place(fellow, read):
        def some(u, carry):
            for g in range(per_den):
                num = read(u * (per_den // per_pack) + g // per_pack).astype(F32)
                den = read(num_packs + u).astype(F32)
                num = roll(num, -width * (g % per_pack))
                den = roll(den, width - half * g)
                joined = jnp.where(lane < width, num, jnp.where(lane < width + half, den, 0.0))
                weights_ref[fellow * particles + u * per_den + g] = jnp.concatenate(
                    [joined, zero_tail], axis=0
                ).astype(BF16)
            return carry

        lax.fori_loop(0, particles // per_den, some, 0)

    def tabulate(owner, read):
        for t in range(slots):
            ref = roll(read(t // per_pack).astype(F32), -width * (t % per_pack))
            square = ref * ref
            power = (square + roll(square, -half)).astype(BF16).astype(F32) * -0.5
            power = roll(power, width)
            joined = jnp.where(lane < width, ref, jnp.where(lane < width + half, power, 0.0))
            table[owner * slots + t] = jnp.concatenate(
                [joined, jnp.zeros((tall_rows - angles, LANES), F32)], axis=0
            ).astype(BF16)

    place(my_fellow, lambda u: w_ref[my_fellow, u])
    tabulate(my_owner, lambda u: r_ref[u])
    own_rows.wait()
    for copy in row_copies:
        copy.wait_recv()
    to_smem = pltpu.make_async_copy(tall, rows_ref, own_sem.at[1])
    to_smem.start()
    for step in range(1, max(owners, fellows)):
        if step < fellows:
            image_copies[step - 1].wait_recv()
            source = lax.rem(my_fellow + fellows - step, fellows)
            place(source, lambda u: wall[source, u])
        if step < owners:
            ref_copies[step - 1].wait_recv()
            holder = lax.rem(my_owner + owners - step, owners)
            tabulate(holder, lambda u: rall[holder, u])
    to_smem.wait()

    batch = 8

    def score(fellow, begin):
        lows = []
        highs = []
        for k in range(batch):
            i = begin + k
            refs = jnp.concatenate([table[rows_ref[fellow, i, j]] for j in range(top)], axis=0)
            grid = lax.dot_general(
                refs,
                weights_ref[fellow * particles + i],
                (((1,), (1,)), ((), ())),
                preferred_element_type=F32,
            )
            for j in range(top):
                base = j * tall_rows
                lo = grid[base : base + 8]
                for tile in range(1, cut // 8):
                    lo = lo + roll(grid[base + 8 * tile : base + 8 * tile + 8], 8 * tile)
                hi = grid[base + cut : base + cut + 8]
                for tile in range(cut // 8 + 1, tiles):
                    hi = hi + roll(grid[base + 8 * tile : base + 8 * tile + 8], 8 * tile - cut)
                lo = pltpu.roll(lo, 0, 1, stride=1, stride_axis=0)
                hi = pltpu.roll(hi, 0, 1, stride=1, stride_axis=0)
                lows.append(jnp.sum(lo, axis=0, keepdims=True))
                highs.append(jnp.sum(hi, axis=0, keepdims=True))
        rows = batch * top
        start = pl.multiple_of(begin * top, rows)
        low[pl.ds(start, rows)] = jnp.concatenate(lows, axis=0)
        high[pl.ds(start, rows)] = jnp.concatenate(highs, axis=0)

    part_copies = []
    chunk = particles * top
    for fellow in range(fellows):

        def some(b, carry):
            score(fellow, b * batch)
            return carry

        lax.fori_loop(0, particles // batch, some, 0)
        lo = low[...]
        hi = high[...]
        spot = lane_of(lo.shape)
        total = roll(lo, 1) + jnp.where(spot < cut, roll(lo, 1 - angles), 0.0)
        back = angles - 1 - cut
        total = total + roll(hi, -back) + jnp.where(spot >= cut + 1, roll(hi, cut + 1), 0.0)
        place_at = parts.at[my_fellow, pl.ds(fellow * chunk, chunk)]
        parts[my_fellow, pl.ds(fellow * chunk, chunk)] = jnp.where(spot < angles, total, 0.0)
        for step in range(1, fellows):
            peer = lax.rem(my_fellow + step, fellows)
            copy = remote(place_at, place_at, ls.at[step, fellow], lr.at[step, fellow], "img", peer)
            copy.start()
            part_copies.append(copy)
    for copy in row_copies + ref_copies + image_copies:
        copy.wait_send()
    for copy in part_copies:
        copy.wait()


def group_of(x, top, combine):
    row = lax.broadcasted_iota(jnp.int32, x.shape, 0)
    count = x.shape[0]
    step = 1
    while step < top:
        swapped = jnp.where(
            (row // step) % 2 == 0, pltpu.roll(x, count - step, 0), pltpu.roll(x, step, 0)
        )
        x = combine(x, swapped)
        step *= 2
    return x


def total_kernel(dims, rows_ref, parts, weights_ref, out_ref, acc, ext_lo, ext_hi):
    fellows, particles, owners, slots, top, angles, half = dims
    width = 2 * half
    per_pack = LANES // width
    per_den = LANES // half
    num_packs = slots // per_pack
    cut = (angles // 16) * 8 + (8 if (angles // 8) % 2 else 0)
    tiles = angles // 8
    tall_rows = -(-angles // 16) * 16
    logits = parts[0]
    for fellow in range(1, fellows):
        logits = logits + parts[fellow]
    spot = lane_of(logits.shape)
    inside = spot < angles
    highest = jnp.max(jnp.where(inside, logits, -jnp.inf), axis=1, keepdims=True)
    highest = group_of(jnp.broadcast_to(highest, logits.shape), top, jnp.maximum)
    exponent = jnp.where(inside, jnp.exp(logits - highest), 0.0)
    summed = jnp.sum(exponent, axis=1, keepdims=True)
    summed = group_of(jnp.broadcast_to(summed, logits.shape), top, jnp.add)
    post = (exponent / summed).astype(BF16).astype(F32)
    lo = jnp.where(inside, post, roll(post, LANES - angles))
    hi = jnp.where((spot >= cut) & inside, roll(post, cut), roll(post, cut - angles))
    ext_lo[...] = lo.reshape(ext_lo.shape)
    ext_hi[...] = hi.reshape(ext_hi.shape)
    acc[...] = jnp.zeros_like(acc)

    def pair(m):
        lo_rows = ext_lo[m]
        hi_rows = ext_hi[m]
        for k in range(2):
            i = 2 * m + k
            turned = []
            for j in range(top):
                e = k * top + j
                first = pltpu.roll(
                    jnp.broadcast_to(lo_rows[e : e + 1], (8, LANES)), 0, 1, stride=1, stride_axis=0
                )
                second = pltpu.roll(
                    jnp.broadcast_to(hi_rows[e : e + 1], (8, LANES)), 0, 1, stride=1, stride_axis=0
                )
                for tile in range(tiles):
                    if 8 * tile < cut:
                        turned.append(roll(first, 8 * tile) if tile else first)
                    else:
                        shift = 8 * tile - cut
                        turned.append(roll(second, shift) if shift else second)
                for tile in range(tiles, tall_rows // 8):
                    turned.append(second)
            circle = jnp.concatenate(turned, axis=0).astype(BF16)
            grid = jnp.dot(circle, weights_ref[i], preferred_element_type=F32)
            held = [acc[rows_ref[i, j]] for j in range(top)]
            for j in range(top):
                acc[rows_ref[i, j]] = held[j] + grid[j * tall_rows : j * tall_rows + angles]

    def some(b, carry):
        for m in range(batch // 2):
            pair(b * (batch // 2) + m)
        return carry

    batch = 8
    lax.fori_loop(0, ext_lo.shape[0] // (batch // 2), some, 0)
    lane = lane_of((angles, LANES))

    def pack(owner, carry):
        nums = [None] * num_packs
        dens = [None] * (slots // per_den)
        for t in range(slots):
            value = acc[owner * slots + t]
            g, u = t % per_pack, t // per_pack
            num = roll(value, width * g)
            nums[u] = num if g == 0 else jnp.where(lane >= width * g, num, nums[u])
            h, v = t % per_den, t // per_den
            den = roll(value, half * h - width)
            dens[v] = den if h == 0 else jnp.where(lane >= half * h, den, dens[v])
        for u, value in enumerate(nums + dens):
            out_ref[owner, u] = value.astype(BF16)
        return carry

    lax.fori_loop(0, owners, pack, 0)


def gather_kernel(axis, size, x_ref, out_ref, landed, send, recv):
    me = lax.axis_index(axis)
    greet(((axis, size),))
    copies = []
    for step in range(1, size):
        peer = lax.rem(me + step, size)
        copies.append(
            pltpu.make_async_remote_copy(
                src_ref=x_ref.at[peer],
                dst_ref=landed.at[step - 1],
                send_sem=send.at[step],
                recv_sem=recv.at[step],
                device_id={axis: peer},
                device_id_type=MESH,
            )
        )
    for copy in copies:
        copy.start()
    total = x_ref[me].astype(F32)
    for step in range(1, size):
        copies[step - 1].wait_recv()
        total = total + landed[step - 1].astype(F32)
    out_ref[...] = total
    for copy in copies:
        copy.wait_send()


def on_device(images, ctf, classes, class_place, references, sigma2):
    shells = sigma2.shape[0]
    angles = ctf.shape[1] // shells
    particles = images.shape[0]
    per_owner = references.shape[0]
    top = classes.shape[1]
    owners = lax.axis_size("cls")
    fellows = lax.axis_size("img")
    my_fellow = lax.axis_index("img")
    half = shells // fellows
    width = 2 * half
    per_pack = LANES // width
    per_den = LANES // half
    slots = -(-per_owner // per_den) * per_den
    dims = (fellows, particles, owners, slots, top, angles, half)

    scaling = ctf.astype(F32).reshape(particles, shells, angles) * (1.0 / sigma2)[None, :, None]
    weighted = (
        images.astype(F32).reshape(particles, shells, 2, angles) * scaling[:, :, None, :]
    ).astype(BF16)
    ctf_power = (ctf.astype(F32).reshape(particles, shells, angles) * scaling).astype(BF16)
    num = weighted.reshape(particles // per_pack, per_pack, fellows, half, 2, angles)
    num = num.transpose(2, 0, 5, 1, 4, 3).reshape(fellows, -1, angles, LANES)
    den = ctf_power.reshape(particles // per_den, per_den, fellows, half, angles)
    den = den.transpose(2, 0, 4, 1, 3).reshape(fellows, -1, angles, LANES)
    send = jnp.concatenate([num, den], axis=1)
    mine = lax.dynamic_slice_in_dim(references, my_fellow * (width * angles), width * angles, 1)
    mine = jnp.pad(mine, ((0, slots - per_owner), (0, 0)))
    mine = mine.reshape(slots // per_pack, per_pack, half, 2, angles)[..., ::-1]
    mine = mine.transpose(0, 4, 1, 3, 2).reshape(-1, angles, LANES)

    lookup = classes[:, :, None] == jnp.arange(class_place.shape[0], dtype=jnp.int32)[None, None, :]
    table_rows = jnp.sum(jnp.where(lookup, class_place[None, None, :], 0), axis=2)
    rows = (table_rows // per_owner) * slots + table_rows % per_owner
    rows = jnp.pad(rows, ((0, 0), (0, LANES - top)))

    packs = send.shape[1]
    everyone = fellows * particles
    tall_rows = -(-angles // 16) * 16
    pairs = everyone // 2
    smem = pl.BlockSpec(memory_space=pltpu.SMEM)
    dma = pltpu.SemaphoreType.DMA
    parts, weights, tall = pl.pallas_call(
        functools.partial(score_kernel, dims),
        out_shape=(
            jax.ShapeDtypeStruct((fellows, everyone * top, LANES), F32),
            jax.ShapeDtypeStruct((everyone, LANES, LANES), BF16),
            jax.ShapeDtypeStruct((fellows, particles, LANES), jnp.int32),
        ),
        in_specs=vmem_specs(3),
        out_specs=tuple(vmem_specs(3)),
        scratch_shapes=[
            VMEM((fellows, packs, angles, LANES), BF16),
            VMEM((owners,) + mine.shape, BF16),
            pltpu.SMEM((fellows, particles, LANES), jnp.int32),
            VMEM((owners * slots, tall_rows, LANES), BF16),
            VMEM((particles * top, LANES), F32),
            VMEM((particles * top, LANES), F32),
            dma((2,)),
            dma((fellows,)),
            dma((fellows,)),
            dma((owners,)),
            dma((owners,)),
            dma((fellows,)),
            dma((fellows,)),
            dma((fellows, fellows)),
            dma((fellows, fellows)),
        ],
        compiler_params=pltpu.CompilerParams(collective_id=0, has_side_effects=True),
    )(send, mine, rows)
    row_list = tall[:, :, :top].reshape(everyone, top)
    sums = pl.pallas_call(
        functools.partial(total_kernel, dims),
        out_shape=jax.ShapeDtypeStruct(
            (owners, slots // per_pack + slots // per_den, angles, LANES), BF16
        ),
        in_specs=[smem] + vmem_specs(2),
        out_specs=pl.BlockSpec(memory_space=pltpu.VMEM),
        scratch_shapes=[
            VMEM((owners * slots, angles, LANES), F32),
            VMEM((pairs, 2 * top, LANES), F32),
            VMEM((pairs, 2 * top, LANES), F32),
        ],
    )(row_list, parts, weights)
    share = pl.pallas_call(
        functools.partial(gather_kernel, "cls", owners),
        out_shape=jax.ShapeDtypeStruct(sums.shape[1:], F32),
        in_specs=vmem_specs(1),
        out_specs=pl.BlockSpec(memory_space=pltpu.VMEM),
        scratch_shapes=[
            VMEM((owners - 1,) + sums.shape[1:], BF16),
            pltpu.SemaphoreType.DMA((owners,)),
            pltpu.SemaphoreType.DMA((owners,)),
        ],
        compiler_params=pltpu.CompilerParams(collective_id=2, has_side_effects=True),
    )(sums)
    num_packs = slots // per_pack
    num = share[:num_packs].reshape(num_packs, angles, per_pack, 2, half)
    num = num.transpose(0, 2, 4, 3, 1).reshape(slots, half, 2, angles)[:per_owner]
    den = share[num_packs:].reshape(-1, angles, per_den, half)
    den = den.transpose(0, 2, 3, 1).reshape(slots, half, 1, angles)[:per_owner]
    return (num / (den + 1.0)).reshape(per_owner, -1)


def solution(mesh):
    in_specs = (
        P(("cls", "img"), None),
        P(("cls", "img"), None),
        P(("cls", "img"), None),
        P(),
        P("cls", None),
        P(),
    )
    out_specs = P("cls", "img")
    return jax.shard_map(
        on_device, mesh=mesh, in_specs=in_specs, out_specs=out_specs, check_vma=False
    )
```

```python
import functools

import jax
import jax.numpy as jnp
from jax import lax
from jax.experimental import pallas as pl
from jax.experimental.pallas import tpu as pltpu
from jax.sharding import PartitionSpec as P

MESH = pl.DeviceIdType.MESH
VMEM = pltpu.VMEM
F32 = jnp.float32
BF16 = jnp.bfloat16
LANES = 128


def vmem_specs(count):
    return [pl.BlockSpec(memory_space=pltpu.VMEM)] * count


def greet(groups):
    barrier = pltpu.get_barrier_semaphore()
    total = 0
    for axis, size in groups:
        me = lax.axis_index(axis)
        for step in range(1, size):
            peer = lax.rem(me + step, size)
            pl.semaphore_signal(barrier, inc=1, device_id={axis: peer}, device_id_type=MESH)
            total += 1
    pl.semaphore_wait(barrier, total)


def lane_of(shape):
    return lax.broadcasted_iota(jnp.int32, shape, len(shape) - 1)


def roll(x, shift):
    return pltpu.roll(x, shift % LANES, x.ndim - 1)


def score_kernel(
    dims, place_ref, w_ref, r_ref, t_ref, sigma_ref, parts, weights_ref, tall, wall, rall, rows_ref,
    table, low, high, pick_num, pick_den,
    own_sem, ws, wr, rs, rr, ts, tr, ls, lr,
):
    fellows, particles, owners, per_owner, slots, top, angles, half = dims
    width = 2 * half
    per_pack = LANES // width
    per_den = LANES // half
    tall_rows = table.shape[1]
    num_packs = particles // per_pack
    tiles = angles // 8
    cut = (tiles // 2 + tiles % 2) * 8
    my_owner = lax.axis_index("cls")
    my_fellow = lax.axis_index("img")
    greet((("cls", owners), ("img", fellows)))

    def remote(src, dst, send, recv, axis, peer):
        return pltpu.make_async_remote_copy(
            src_ref=src,
            dst_ref=dst,
            send_sem=send,
            recv_sem=recv,
            device_id={axis: peer},
            device_id_type=MESH,
        )

    row_copies = []
    ref_copies = []
    image_copies = []
    for step in range(1, fellows):
        peer = lax.rem(my_fellow + step, fellows)
        row_copies.append(remote(t_ref, tall.at[my_fellow], ts.at[step], tr.at[step], "img", peer))
        image_copies.append(
            remote(w_ref.at[peer], wall.at[my_fellow], ws.at[step], wr.at[step], "img", peer)
        )
    for step in range(1, owners):
        peer = lax.rem(my_owner + step, owners)
        ref_copies.append(remote(r_ref, rall.at[my_owner], rs.at[step], rr.at[step], "cls", peer))
    for copy in row_copies + ref_copies + image_copies:
        copy.start()
    own_rows = pltpu.make_async_copy(t_ref, tall.at[my_fellow], own_sem.at[0])
    own_rows.start()

    lane = lane_of((angles, LANES))
    zero_tail = jnp.zeros((LANES - angles, LANES), F32)
    source_lane = lax.broadcasted_iota(jnp.int32, (LANES, LANES), 0)
    target_lane = lax.broadcasted_iota(jnp.int32, (LANES, LANES), 1)
    shell = target_lane % half
    num_source = jnp.where(target_lane < width, 2 * shell + target_lane // half, -LANES)
    for g in range(per_pack):
        pick_num[g] = (source_lane == num_source + width * g).astype(F32).astype(BF16)
    den_source = jnp.where(target_lane < width + half, shell, -LANES)
    for g in range(per_den):
        pick_den[g] = (source_lane == den_source + half * g).astype(F32).astype(BF16)
    spread = jnp.concatenate([1.0 / sigma_ref[...]] * (LANES // sigma_ref.shape[1]), axis=1)
    spread = jnp.broadcast_to(spread, (8, LANES))
    row_lane = lane_of((8, LANES))
    inverse = jnp.zeros((8, LANES), F32)
    for part in range(3):
        shift = lax.rem(half * part - half * my_fellow + LANES, LANES)
        inverse = jnp.where(row_lane // half == part, pltpu.roll(spread, shift, 1), inverse)
    inverse = inverse[0:1]

    def place(fellow, read):
        def some(u, carry):
            for g in range(per_den):
                num = jnp.dot(
                    read(u * (per_den // per_pack) + g // per_pack),
                    pick_num[g % per_pack],
                    preferred_element_type=F32,
                )
                den = jnp.dot(read(num_packs + u), pick_den[g], preferred_element_type=F32)
                joined = jnp.where(lane < width, num, den) * (den * inverse)
                weights_ref[fellow * particles + u * per_den + g] = jnp.concatenate(
                    [joined, zero_tail], axis=0
                ).astype(BF16)
            return carry

        lax.fori_loop(0, particles // per_den, some, 0)

    def tabulate(owner, read):
        for t in range(per_owner):
            ref = jnp.dot(read(t // per_pack), pick_num[t % per_pack], preferred_element_type=F32)
            square = ref * ref
            power = (square + roll(square, -half)).astype(BF16).astype(F32) * -0.5
            power = roll(power, width)
            joined = jnp.where(lane < width, ref, jnp.where(lane < width + half, power, 0.0))
            table[owner * per_owner + t] = jnp.concatenate(
                [joined, jnp.zeros((tall_rows - angles, LANES), F32)], axis=0
            ).astype(BF16)

    place(my_fellow, lambda u: w_ref[my_fellow, u])
    tabulate(my_owner, lambda u: r_ref[u])
    own_rows.wait()
    for copy in row_copies:
        copy.wait_recv()
    to_smem = pltpu.make_async_copy(tall, rows_ref, own_sem.at[1])
    to_smem.start()
    for step in range(1, max(owners, fellows)):
        if step < fellows:
            image_copies[step - 1].wait_recv()
            source = lax.rem(my_fellow + fellows - step, fellows)
            place(source, lambda u: wall[source, u])
        if step < owners:
            ref_copies[step - 1].wait_recv()
            holder = lax.rem(my_owner + owners - step, owners)
            tabulate(holder, lambda u: rall[holder, u])
    to_smem.wait()

    batch = 8

    def score(fellow, begin):
        lows = []
        highs = []
        for k in range(batch):
            i = begin + k
            refs = jnp.concatenate([table[place_ref[rows_ref[fellow, i, j]]] for j in range(top)], axis=0)
            grid = lax.dot_general(
                refs,
                weights_ref[fellow * particles + i],
                (((1,), (1,)), ((), ())),
                preferred_element_type=F32,
            )
            for j in range(top):
                base = j * tall_rows
                lo = grid[base : base + 8]
                for tile in range(1, cut // 8):
                    lo = lo + roll(grid[base + 8 * tile : base + 8 * tile + 8], 8 * tile)
                hi = grid[base + cut : base + cut + 8]
                for tile in range(cut // 8 + 1, tiles):
                    hi = hi + roll(grid[base + 8 * tile : base + 8 * tile + 8], 8 * tile - cut)
                lo = pltpu.roll(lo, 0, 1, stride=1, stride_axis=0)
                hi = pltpu.roll(hi, 0, 1, stride=1, stride_axis=0)
                lows.append(jnp.sum(lo, axis=0, keepdims=True))
                highs.append(jnp.sum(hi, axis=0, keepdims=True))
        rows = batch * top
        start = pl.multiple_of(begin * top, rows)
        low[pl.ds(start, rows)] = jnp.concatenate(lows, axis=0)
        high[pl.ds(start, rows)] = jnp.concatenate(highs, axis=0)

    part_copies = []
    chunk = particles * top
    for fellow in range(fellows):

        def some(b, carry):
            score(fellow, b * batch)
            return carry

        lax.fori_loop(0, particles // batch, some, 0)
        lo = low[...]
        hi = high[...]
        spot = lane_of(lo.shape)
        total = roll(lo, 1) + jnp.where(spot < cut, roll(lo, 1 - angles), 0.0)
        back = angles - 1 - cut
        total = total + roll(hi, -back) + jnp.where(spot >= cut + 1, roll(hi, cut + 1), 0.0)
        place_at = parts.at[my_fellow, pl.ds(fellow * chunk, chunk)]
        parts[my_fellow, pl.ds(fellow * chunk, chunk)] = jnp.where(spot < angles, total, 0.0)
        for step in range(1, fellows):
            peer = lax.rem(my_fellow + step, fellows)
            copy = remote(place_at, place_at, ls.at[step, fellow], lr.at[step, fellow], "img", peer)
            copy.start()
            part_copies.append(copy)
    for copy in row_copies + ref_copies + image_copies:
        copy.wait_send()
    for copy in part_copies:
        copy.wait()


def group_of(x, top, combine):
    row = lax.broadcasted_iota(jnp.int32, x.shape, 0)
    count = x.shape[0]
    step = 1
    while step < top:
        swapped = jnp.where(
            (row // step) % 2 == 0, pltpu.roll(x, count - step, 0), pltpu.roll(x, step, 0)
        )
        x = combine(x, swapped)
        step *= 2
    return x


def total_kernel(dims, place_ref, rows_ref, parts, weights_ref, out_ref, acc, ext_lo, ext_hi):
    fellows, particles, owners, per_owner, slots, top, angles, half = dims
    width = 2 * half
    per_pack = LANES // width
    per_den = LANES // half
    num_packs = slots // per_pack
    cut = (angles // 16) * 8 + (8 if (angles // 8) % 2 else 0)
    tiles = angles // 8
    tall_rows = -(-angles // 16) * 16
    logits = parts[0]
    for fellow in range(1, fellows):
        logits = logits + parts[fellow]
    spot = lane_of(logits.shape)
    inside = spot < angles
    highest = jnp.max(jnp.where(inside, logits, -jnp.inf), axis=1, keepdims=True)
    highest = group_of(jnp.broadcast_to(highest, logits.shape), top, jnp.maximum)
    exponent = jnp.where(inside, jnp.exp(logits - highest), 0.0)
    summed = jnp.sum(exponent, axis=1, keepdims=True)
    summed = group_of(jnp.broadcast_to(summed, logits.shape), top, jnp.add)
    post = (exponent / summed).astype(BF16).astype(F32)
    lo = jnp.where(inside, post, roll(post, LANES - angles))
    hi = jnp.where((spot >= cut) & inside, roll(post, cut), roll(post, cut - angles))
    ext_lo[...] = lo.reshape(ext_lo.shape)
    ext_hi[...] = hi.reshape(ext_hi.shape)
    acc[...] = jnp.zeros_like(acc)

    def pair(m):
        lo_rows = ext_lo[m]
        hi_rows = ext_hi[m]
        for k in range(2):
            i = 2 * m + k
            turned = []
            for j in range(top):
                e = k * top + j
                first = pltpu.roll(
                    jnp.broadcast_to(lo_rows[e : e + 1], (8, LANES)), 0, 1, stride=1, stride_axis=0
                )
                second = pltpu.roll(
                    jnp.broadcast_to(hi_rows[e : e + 1], (8, LANES)), 0, 1, stride=1, stride_axis=0
                )
                for tile in range(tiles):
                    if 8 * tile < cut:
                        turned.append(roll(first, 8 * tile) if tile else first)
                    else:
                        shift = 8 * tile - cut
                        turned.append(roll(second, shift) if shift else second)
                for tile in range(tiles, tall_rows // 8):
                    turned.append(second)
            circle = jnp.concatenate(turned, axis=0).astype(BF16)
            grid = jnp.dot(circle, weights_ref[i], preferred_element_type=F32)
            spots = [place_ref[rows_ref[i, j]] for j in range(top)]
            held = [acc[spot] for spot in spots]
            for j in range(top):
                acc[spots[j]] = held[j] + grid[j * tall_rows : j * tall_rows + angles]

    def some(b, carry):
        for m in range(batch // 2):
            pair(b * (batch // 2) + m)
        return carry

    batch = 8
    lax.fori_loop(0, ext_lo.shape[0] // (batch // 2), some, 0)
    lane = lane_of((angles, LANES))

    def pack(owner, carry):
        nums = [None] * num_packs
        dens = [None] * -(-slots // per_den)
        for t in range(per_owner):
            value = acc[owner * per_owner + t]
            g, u = t % per_pack, t // per_pack
            num = roll(value, width * g)
            nums[u] = num if g == 0 else jnp.where(lane >= width * g, num, nums[u])
            h, v = t % per_den, t // per_den
            den = roll(value, half * h - width)
            dens[v] = den if h == 0 else jnp.where(lane >= half * h, den, dens[v])
        for u, value in enumerate(nums + dens):
            out_ref[owner, u] = value.astype(BF16)
        return carry

    lax.fori_loop(0, owners, pack, 0)


def gather_kernel(axis, size, half, slots, x_ref, out_ref, landed, send, recv):
    me = lax.axis_index(axis)
    greet(((axis, size),))
    copies = []
    for step in range(1, size):
        peer = lax.rem(me + step, size)
        copies.append(
            pltpu.make_async_remote_copy(
                src_ref=x_ref.at[peer],
                dst_ref=landed.at[step - 1],
                send_sem=send.at[step],
                recv_sem=recv.at[step],
                device_id={axis: peer},
                device_id_type=MESH,
            )
        )
    for copy in copies:
        copy.start()
    total = x_ref[me].astype(F32)
    for step in range(1, size):
        copies[step - 1].wait_recv()
        total = total + landed[step - 1].astype(F32)
    width = 2 * half
    per_pack = LANES // width
    num_packs = slots // per_pack
    target = lax.broadcasted_iota(jnp.int32, (LANES, LANES), 0)
    source = lax.broadcasted_iota(jnp.int32, (LANES, LANES), 1)
    shell = (target % width) // 2
    flip = target - target % width + (target % 2) * half + shell

    def picked(wanted, x):
        return lax.dot_general(
            (source == wanted).astype(F32),
            x,
            (((1,), (1,)), ((), ())),
            precision=lax.Precision.HIGHEST,
            preferred_element_type=F32,
        )

    for u in range(num_packs):
        held = num_packs + (u * per_pack * half) // LANES
        offset = (u * per_pack * half) % LANES
        den = picked(offset + half * (target // width) + shell, total[held])
        out_ref[u] = picked(flip, total[u]) / (den + 1.0)
    for copy in copies:
        copy.wait_send()


def on_device(images, ctf, classes, class_place, references, sigma2):
    shells = sigma2.shape[0]
    angles = ctf.shape[1] // shells
    particles = images.shape[0]
    per_owner = references.shape[0]
    top = classes.shape[1]
    owners = lax.axis_size("cls")
    fellows = lax.axis_size("img")
    my_fellow = lax.axis_index("img")
    half = shells // fellows
    width = 2 * half
    per_pack = LANES // width
    per_den = LANES // half
    slots = -(-per_owner // per_pack) * per_pack
    dims = (fellows, particles, owners, per_owner, slots, top, angles, half)

    num = images.reshape(particles // per_pack, per_pack, fellows, width, angles)
    num = num.transpose(2, 0, 4, 1, 3).reshape(fellows, -1, angles, LANES)
    den = ctf.reshape(particles // per_den, per_den, fellows, half, angles)
    den = den.transpose(2, 0, 4, 1, 3).reshape(fellows, -1, angles, LANES)
    send = jnp.concatenate([num, den], axis=1)
    mine = lax.dynamic_slice_in_dim(references, my_fellow * (width * angles), width * angles, 1)
    mine = jnp.pad(mine, ((0, slots - per_owner), (0, 0)))
    mine = mine.reshape(slots // per_pack, per_pack, width, angles)[..., ::-1]
    mine = mine.transpose(0, 3, 1, 2).reshape(-1, angles, LANES)
    rows = jnp.pad(classes, ((0, 0), (0, LANES - top)))

    packs = send.shape[1]
    everyone = fellows * particles
    tall_rows = -(-angles // 16) * 16
    pairs = everyone // 2
    smem = pl.BlockSpec(memory_space=pltpu.SMEM)
    dma = pltpu.SemaphoreType.DMA
    parts, weights, tall = pl.pallas_call(
        functools.partial(score_kernel, dims),
        out_shape=(
            jax.ShapeDtypeStruct((fellows, everyone * top, LANES), F32),
            jax.ShapeDtypeStruct((everyone, LANES, LANES), BF16),
            jax.ShapeDtypeStruct((fellows, particles, LANES), jnp.int32),
        ),
        in_specs=[smem] + vmem_specs(4),
        out_specs=tuple(vmem_specs(3)),
        scratch_shapes=[
            VMEM((fellows, packs, angles, LANES), BF16),
            VMEM((owners,) + mine.shape, BF16),
            pltpu.SMEM((fellows, particles, LANES), jnp.int32),
            VMEM((owners * per_owner, tall_rows, LANES), BF16),
            VMEM((particles * top, LANES), F32),
            VMEM((particles * top, LANES), F32),
            VMEM((per_pack, LANES, LANES), BF16),
            VMEM((per_den, LANES, LANES), BF16),
            dma((2,)),
            dma((fellows,)),
            dma((fellows,)),
            dma((owners,)),
            dma((owners,)),
            dma((fellows,)),
            dma((fellows,)),
            dma((fellows, fellows)),
            dma((fellows, fellows)),
        ],
        compiler_params=pltpu.CompilerParams(collective_id=0, has_side_effects=True),
    )(class_place, send, mine, rows, sigma2.reshape(1, shells))
    row_list = tall[:, :, :top].reshape(everyone, top)
    sums = pl.pallas_call(
        functools.partial(total_kernel, dims),
        out_shape=jax.ShapeDtypeStruct(
            (owners, slots // per_pack - (-slots // per_den), angles, LANES), BF16
        ),
        in_specs=[smem, smem] + vmem_specs(2),
        out_specs=pl.BlockSpec(memory_space=pltpu.VMEM),
        scratch_shapes=[
            VMEM((owners * per_owner, angles, LANES), F32),
            VMEM((pairs, 2 * top, LANES), F32),
            VMEM((pairs, 2 * top, LANES), F32),
        ],
    )(class_place, row_list, parts, weights)
    share = pl.pallas_call(
        functools.partial(gather_kernel, "cls", owners, half, slots),
        out_shape=jax.ShapeDtypeStruct((slots // per_pack, LANES, angles), F32),
        in_specs=vmem_specs(1),
        out_specs=pl.BlockSpec(memory_space=pltpu.VMEM),
        scratch_shapes=[
            VMEM((owners - 1,) + sums.shape[1:], BF16),
            pltpu.SemaphoreType.DMA((owners,)),
            pltpu.SemaphoreType.DMA((owners,)),
        ],
        compiler_params=pltpu.CompilerParams(collective_id=2, has_side_effects=True),
    )(sums)
    return share.reshape(slots * width, angles)[: per_owner * width].reshape(per_owner, -1)


def solution(mesh):
    in_specs = (
        P(("cls", "img"), None),
        P(("cls", "img"), None),
        P(("cls", "img"), None),
        P(),
        P("cls", None),
        P(),
    )
    out_specs = P("cls", "img")
    return jax.shard_map(
        on_device, mesh=mesh, in_specs=in_specs, out_specs=out_specs, check_vma=False
    )
```

```python
import functools

import jax
import jax.numpy as jnp
from jax import lax
from jax.experimental import pallas as pl
from jax.experimental.pallas import tpu as pltpu
from jax.sharding import PartitionSpec as P

MESH = pl.DeviceIdType.MESH
VMEM = pltpu.VMEM
F32 = jnp.float32
BF16 = jnp.bfloat16
LANES = 128


def vmem_specs(count):
    return [pl.BlockSpec(memory_space=pltpu.VMEM)] * count


def greet(groups):
    barrier = pltpu.get_barrier_semaphore()
    total = 0
    for axis, size in groups:
        me = lax.axis_index(axis)
        for step in range(1, size):
            peer = lax.rem(me + step, size)
            pl.semaphore_signal(barrier, inc=1, device_id={axis: peer}, device_id_type=MESH)
            total += 1
    pl.semaphore_wait(barrier, total)


def lane_of(shape):
    return lax.broadcasted_iota(jnp.int32, shape, len(shape) - 1)


def roll(x, shift):
    return pltpu.roll(x, shift % LANES, x.ndim - 1)


def score_kernel(
    dims, place_ref, n_ref, d_ref, r_ref, t_ref, sigma_ref, parts, weights_ref, tall, nall, dall,
    rall, rows_ref,
    table, low, high, pick_num, pick_den,
    own_sem, ns, nr, ds, dr, rs, rr, fs, fr, ts, tr, ls, lr,
):
    fellows, particles, owners, per_owner, slots, top, angles, half = dims
    width = 2 * half
    per_pack = LANES // width
    per_den = LANES // half
    tall_rows = table.shape[1]
    tiles = angles // 8
    cut = (tiles // 2 + tiles % 2) * 8
    my_owner = lax.axis_index("cls")
    my_fellow = lax.axis_index("img")
    greet((("cls", owners), ("img", fellows)))

    def remote(src, dst, send, recv, axis, peer):
        return pltpu.make_async_remote_copy(
            src_ref=src,
            dst_ref=dst,
            send_sem=send,
            recv_sem=recv,
            device_id={axis: peer},
            device_id_type=MESH,
        )

    row_copies = []
    ref_copies = []
    image_copies = []
    for step in range(1, fellows):
        peer = lax.rem(my_fellow + step, fellows)
        row_copies.append(remote(t_ref, tall.at[my_fellow], ts.at[step], tr.at[step], "img", peer))
        image_copies.append(
            (
                remote(n_ref.at[peer], nall.at[my_fellow], ns.at[step], nr.at[step], "img", peer),
                remote(d_ref.at[peer], dall.at[my_fellow], ds.at[step], dr.at[step], "img", peer),
            )
        )
    partner = my_owner + 1 - 2 * lax.rem(my_owner, 2)
    strides = owners // 2
    for step in range(1, strides):
        peer = lax.rem(my_owner + 2 * step, owners)
        ref_copies.append(remote(r_ref, rall.at[my_owner], rs.at[step], rr.at[step], "cls", peer))
    forwards = [remote(r_ref, rall.at[my_owner], fs.at[0], fr.at[0], "cls", partner)]
    for copy in ref_copies[::-1] + forwards + row_copies:
        copy.start()
    for num_copy, den_copy in image_copies:
        num_copy.start()
        den_copy.start()
    own_rows = pltpu.make_async_copy(t_ref, tall.at[my_fellow], own_sem.at[0])
    own_rows.start()

    lane = lane_of((angles, LANES))
    zero_tail = jnp.zeros((LANES - angles, LANES), F32)
    source_lane = lax.broadcasted_iota(jnp.int32, (LANES, LANES), 0)
    target_lane = lax.broadcasted_iota(jnp.int32, (LANES, LANES), 1)
    shell = target_lane % half
    num_source = jnp.where(target_lane < width, 2 * shell + target_lane // half, -LANES)
    for g in range(per_pack):
        pick_num[g] = (source_lane == num_source + width * g).astype(F32).astype(BF16)
    den_source = jnp.where(target_lane < width + half, shell, -LANES)
    for g in range(per_den):
        pick_den[g] = (source_lane == den_source + half * g).astype(F32).astype(BF16)
    spread = jnp.concatenate([1.0 / sigma_ref[...]] * (LANES // sigma_ref.shape[1]), axis=1)
    spread = jnp.broadcast_to(spread, (8, LANES))
    row_lane = lane_of((8, LANES))
    inverse = jnp.zeros((8, LANES), F32)
    for part in range(3):
        shift = lax.rem(half * part - half * my_fellow + LANES, LANES)
        inverse = jnp.where(row_lane // half == part, pltpu.roll(spread, shift, 1), inverse)
    inverse = inverse[0:1]

    def place(fellow, read_num, read_den):
        def some(u, carry):
            for g in range(per_den):
                num = jnp.dot(
                    read_num(u * (per_den // per_pack) + g // per_pack),
                    pick_num[g % per_pack],
                    preferred_element_type=F32,
                )
                den = jnp.dot(read_den(u), pick_den[g], preferred_element_type=F32)
                joined = jnp.where(lane < width, num, den) * (den * inverse)
                weights_ref[fellow * particles + u * per_den + g] = jnp.concatenate(
                    [joined, zero_tail], axis=0
                ).astype(BF16)
            return carry

        lax.fori_loop(0, particles // per_den, some, 0)

    def tabulate(owner, read):
        for t in range(per_owner):
            ref = jnp.dot(read(t // per_pack), pick_num[t % per_pack], preferred_element_type=F32)
            square = ref * ref
            power = (square + roll(square, -half)).astype(BF16).astype(F32) * -0.5
            power = roll(power, width)
            joined = jnp.where(lane < width, ref, jnp.where(lane < width + half, power, 0.0))
            table[owner * per_owner + t] = jnp.concatenate(
                [joined, jnp.zeros((tall_rows - angles, LANES), F32)], axis=0
            ).astype(BF16)

    tabulate(my_owner, lambda u: r_ref[u])
    for step in range(1, strides):
        holder = lax.rem(my_owner + owners - 2 * step, owners)
        ref_copies[step - 1].wait_recv()
        forward = remote(rall.at[holder], rall.at[holder], fs.at[step], fr.at[step], "cls", partner)
        forward.start()
        forwards.append(forward)
        tabulate(holder, lambda u: rall[holder, u])
    own_rows.wait()
    for copy in row_copies:
        copy.wait_recv()
    to_smem = pltpu.make_async_copy(tall, rows_ref, own_sem.at[1])
    to_smem.start()
    place(my_fellow, lambda u: n_ref[my_fellow, u], lambda u: d_ref[my_fellow, u])
    for step in range(max(strides, fellows)):
        if step < strides:
            forwards[step].wait_recv()
            holder = lax.rem(partner + owners - 2 * step, owners)
            tabulate(holder, lambda u: rall[holder, u])
        if 0 < step < fellows:
            for copy in image_copies[step - 1]:
                copy.wait_recv()
            source = lax.rem(my_fellow + fellows - step, fellows)
            place(source, lambda u: nall[source, u], lambda u: dall[source, u])
    to_smem.wait()

    batch = 8

    def score(fellow, begin):
        lows = []
        highs = []
        for k in range(batch):
            i = begin + k
            refs = jnp.concatenate([table[place_ref[rows_ref[fellow, j, i]]] for j in range(top)], axis=0)
            grid = lax.dot_general(
                refs,
                weights_ref[fellow * particles + i],
                (((1,), (1,)), ((), ())),
                preferred_element_type=F32,
            )
            for j in range(top):
                base = j * tall_rows
                lo = grid[base : base + 8]
                for tile in range(1, cut // 8):
                    lo = lo + roll(grid[base + 8 * tile : base + 8 * tile + 8], 8 * tile)
                hi = grid[base + cut : base + cut + 8]
                for tile in range(cut // 8 + 1, tiles):
                    hi = hi + roll(grid[base + 8 * tile : base + 8 * tile + 8], 8 * tile - cut)
                lo = pltpu.roll(lo, 0, 1, stride=1, stride_axis=0)
                hi = pltpu.roll(hi, 0, 1, stride=1, stride_axis=0)
                lows.append(jnp.sum(lo, axis=0, keepdims=True))
                highs.append(jnp.sum(hi, axis=0, keepdims=True))
        rows = batch * top
        start = pl.multiple_of(begin * top, rows)
        low[pl.ds(start, rows)] = jnp.concatenate(lows, axis=0)
        high[pl.ds(start, rows)] = jnp.concatenate(highs, axis=0)

    part_copies = []
    chunk = particles * top
    for fellow in range(fellows):

        def some(b, carry):
            score(fellow, b * batch)
            return carry

        lax.fori_loop(0, particles // batch, some, 0)
        lo = low[...]
        hi = high[...]
        spot = lane_of(lo.shape)
        total = roll(lo, 1) + jnp.where(spot < cut, roll(lo, 1 - angles), 0.0)
        back = angles - 1 - cut
        total = total + roll(hi, -back) + jnp.where(spot >= cut + 1, roll(hi, cut + 1), 0.0)
        place_at = parts.at[my_fellow, pl.ds(fellow * chunk, chunk)]
        parts[my_fellow, pl.ds(fellow * chunk, chunk)] = jnp.where(spot < angles, total, 0.0)
        for step in range(1, fellows):
            peer = lax.rem(my_fellow + step, fellows)
            copy = remote(place_at, place_at, ls.at[step, fellow], lr.at[step, fellow], "img", peer)
            copy.start()
            part_copies.append(copy)
    for copy in row_copies + ref_copies + forwards:
        copy.wait_send()
    for num_copy, den_copy in image_copies:
        num_copy.wait_send()
        den_copy.wait_send()
    for copy in part_copies:
        copy.wait()


def group_of(x, top, combine):
    row = lax.broadcasted_iota(jnp.int32, x.shape, 0)
    count = x.shape[0]
    step = 1
    while step < top:
        swapped = jnp.where(
            (row // step) % 2 == 0, pltpu.roll(x, count - step, 0), pltpu.roll(x, step, 0)
        )
        x = combine(x, swapped)
        step *= 2
    return x


def total_kernel(dims, place_ref, rows_ref, parts, weights_ref, out_ref, acc, ext_lo, ext_hi):
    fellows, particles, owners, per_owner, slots, top, angles, half = dims
    width = 2 * half
    per_pack = LANES // width
    per_den = LANES // half
    num_packs = slots // per_pack
    cut = (angles // 16) * 8 + (8 if (angles // 8) % 2 else 0)
    tiles = angles // 8
    tall_rows = -(-angles // 16) * 16
    logits = parts[0]
    for fellow in range(1, fellows):
        logits = logits + parts[fellow]
    spot = lane_of(logits.shape)
    inside = spot < angles
    highest = jnp.max(jnp.where(inside, logits, -jnp.inf), axis=1, keepdims=True)
    highest = group_of(jnp.broadcast_to(highest, logits.shape), top, jnp.maximum)
    exponent = jnp.where(inside, jnp.exp(logits - highest), 0.0)
    summed = jnp.sum(exponent, axis=1, keepdims=True)
    summed = group_of(jnp.broadcast_to(summed, logits.shape), top, jnp.add)
    post = (exponent / summed).astype(BF16).astype(F32)
    lo = jnp.where(inside, post, roll(post, LANES - angles))
    hi = jnp.where((spot >= cut) & inside, roll(post, cut), roll(post, cut - angles))
    ext_lo[...] = lo.reshape(ext_lo.shape)
    ext_hi[...] = hi.reshape(ext_hi.shape)
    acc[...] = jnp.zeros_like(acc)

    def pair(m):
        lo_rows = ext_lo[m]
        hi_rows = ext_hi[m]
        for k in range(2):
            i = 2 * m + k
            turned = []
            for j in range(top):
                e = k * top + j
                first = pltpu.roll(
                    jnp.broadcast_to(lo_rows[e : e + 1], (8, LANES)), 0, 1, stride=1, stride_axis=0
                )
                second = pltpu.roll(
                    jnp.broadcast_to(hi_rows[e : e + 1], (8, LANES)), 0, 1, stride=1, stride_axis=0
                )
                for tile in range(tiles):
                    if 8 * tile < cut:
                        turned.append(roll(first, 8 * tile) if tile else first)
                    else:
                        shift = 8 * tile - cut
                        turned.append(roll(second, shift) if shift else second)
                for tile in range(tiles, tall_rows // 8):
                    turned.append(second)
            circle = jnp.concatenate(turned, axis=0).astype(BF16)
            grid = jnp.dot(circle, weights_ref[i], preferred_element_type=F32)
            spots = [
                place_ref[rows_ref[i // particles, j, i % particles]] for j in range(top)
            ]
            held = [acc[spot] for spot in spots]
            for j in range(top):
                acc[spots[j]] = held[j] + grid[j * tall_rows : j * tall_rows + angles]

    def some(b, carry):
        for m in range(batch // 2):
            pair(b * (batch // 2) + m)
        return carry

    batch = 8
    lax.fori_loop(0, ext_lo.shape[0] // (batch // 2), some, 0)
    lane = lane_of((angles, LANES))

    def pack(owner, carry):
        nums = [None] * num_packs
        dens = [None] * -(-slots // per_den)
        for t in range(per_owner):
            value = acc[owner * per_owner + t]
            g, u = t % per_pack, t // per_pack
            num = roll(value, width * g)
            nums[u] = num if g == 0 else jnp.where(lane >= width * g, num, nums[u])
            h, v = t % per_den, t // per_den
            den = roll(value, half * h - width)
            dens[v] = den if h == 0 else jnp.where(lane >= half * h, den, dens[v])
        for u, value in enumerate(nums + dens):
            out_ref[owner, u] = value.astype(BF16)
        return carry

    lax.fori_loop(0, owners, pack, 0)


def gather_kernel(axis, size, half, slots, x_ref, out_ref, landed, send, recv):
    me = lax.axis_index(axis)
    greet(((axis, size),))
    copies = []
    for step in range(1, size):
        peer = lax.rem(me + step, size)
        copies.append(
            pltpu.make_async_remote_copy(
                src_ref=x_ref.at[peer],
                dst_ref=landed.at[step - 1],
                send_sem=send.at[step],
                recv_sem=recv.at[step],
                device_id={axis: peer},
                device_id_type=MESH,
            )
        )
    for copy in copies:
        copy.start()
    total = x_ref[me].astype(F32)
    for step in range(1, size):
        copies[step - 1].wait_recv()
        total = total + landed[step - 1].astype(F32)
    width = 2 * half
    per_pack = LANES // width
    num_packs = slots // per_pack
    target = lax.broadcasted_iota(jnp.int32, (LANES, LANES), 0)
    source = lax.broadcasted_iota(jnp.int32, (LANES, LANES), 1)
    shell = (target % width) // 2
    flip = target - target % width + (target % 2) * half + shell

    def picked(wanted, x):
        return lax.dot_general(
            (source == wanted).astype(F32),
            x,
            (((1,), (1,)), ((), ())),
            precision=lax.Precision.HIGHEST,
            preferred_element_type=F32,
        )

    for u in range(num_packs):
        held = num_packs + (u * per_pack * half) // LANES
        offset = (u * per_pack * half) % LANES
        den = picked(offset + half * (target // width) + shell, total[held])
        out_ref[u] = picked(flip, total[u]) / (den + 1.0)
    for copy in copies:
        copy.wait_send()


def on_device(images, ctf, classes, class_place, references, sigma2):
    shells = sigma2.shape[0]
    angles = ctf.shape[1] // shells
    particles = images.shape[0]
    per_owner = references.shape[0]
    top = classes.shape[1]
    owners = lax.axis_size("cls")
    fellows = lax.axis_size("img")
    my_fellow = lax.axis_index("img")
    half = shells // fellows
    width = 2 * half
    per_pack = LANES // width
    per_den = LANES // half
    slots = -(-per_owner // per_pack) * per_pack
    dims = (fellows, particles, owners, per_owner, slots, top, angles, half)

    num = images.reshape(particles // per_pack, per_pack, fellows, width, angles)
    num = num.transpose(2, 0, 4, 1, 3).reshape(fellows, -1, angles, LANES)
    den = ctf.reshape(particles // per_den, per_den, fellows, half, angles)
    den = den.transpose(2, 0, 4, 1, 3).reshape(fellows, -1, angles, LANES)
    mine = lax.dynamic_slice_in_dim(references, my_fellow * (width * angles), width * angles, 1)
    mine = jnp.pad(mine, ((0, slots - per_owner), (0, 0)))
    mine = mine.reshape(slots // per_pack, per_pack, width, angles)[..., ::-1]
    mine = mine.transpose(0, 3, 1, 2).reshape(-1, angles, LANES)
    rows = classes.T

    everyone = fellows * particles
    tall_rows = -(-angles // 16) * 16
    pairs = everyone // 2
    smem = pl.BlockSpec(memory_space=pltpu.SMEM)
    dma = pltpu.SemaphoreType.DMA
    parts, weights, tall = pl.pallas_call(
        functools.partial(score_kernel, dims),
        out_shape=(
            jax.ShapeDtypeStruct((fellows, everyone * top, LANES), F32),
            jax.ShapeDtypeStruct((everyone, LANES, LANES), BF16),
            jax.ShapeDtypeStruct((fellows, top, particles), jnp.int32),
        ),
        in_specs=[smem] + vmem_specs(5),
        out_specs=tuple(vmem_specs(3)),
        scratch_shapes=[
            VMEM(num.shape, BF16),
            VMEM(den.shape, BF16),
            VMEM((owners,) + mine.shape, BF16),
            pltpu.SMEM((fellows, top, particles), jnp.int32),
            VMEM((owners * per_owner, tall_rows, LANES), BF16),
            VMEM((particles * top, LANES), F32),
            VMEM((particles * top, LANES), F32),
            VMEM((per_pack, LANES, LANES), BF16),
            VMEM((per_den, LANES, LANES), BF16),
            dma((2,)),
            dma((fellows,)),
            dma((fellows,)),
            dma((fellows,)),
            dma((fellows,)),
            dma((owners,)),
            dma((owners,)),
            dma((owners,)),
            dma((owners,)),
            dma((fellows,)),
            dma((fellows,)),
            dma((fellows, fellows)),
            dma((fellows, fellows)),
        ],
        compiler_params=pltpu.CompilerParams(collective_id=0, has_side_effects=True),
    )(class_place, num, den, mine, rows, sigma2.reshape(1, shells))
    sums = pl.pallas_call(
        functools.partial(total_kernel, dims),
        out_shape=jax.ShapeDtypeStruct(
            (owners, slots // per_pack - (-slots // per_den), angles, LANES), BF16
        ),
        in_specs=[smem, smem] + vmem_specs(2),
        out_specs=pl.BlockSpec(memory_space=pltpu.VMEM),
        scratch_shapes=[
            VMEM((owners * per_owner, angles, LANES), F32),
            VMEM((pairs, 2 * top, LANES), F32),
            VMEM((pairs, 2 * top, LANES), F32),
        ],
    )(class_place, tall, parts, weights)
    share = pl.pallas_call(
        functools.partial(gather_kernel, "cls", owners, half, slots),
        out_shape=jax.ShapeDtypeStruct((slots // per_pack, LANES, angles), F32),
        in_specs=vmem_specs(1),
        out_specs=pl.BlockSpec(memory_space=pltpu.VMEM),
        scratch_shapes=[
            VMEM((owners - 1,) + sums.shape[1:], BF16),
            pltpu.SemaphoreType.DMA((owners,)),
            pltpu.SemaphoreType.DMA((owners,)),
        ],
        compiler_params=pltpu.CompilerParams(collective_id=2, has_side_effects=True),
    )(sums)
    return share.reshape(slots * width, angles)[: per_owner * width].reshape(per_owner, -1)


def solution(mesh):
    in_specs = (
        P(("cls", "img"), None),
        P(("cls", "img"), None),
        P(("cls", "img"), None),
        P(),
        P("cls", None),
        P(),
    )
    out_specs = P("cls", "img")
    return jax.shard_map(
        on_device, mesh=mesh, in_specs=in_specs, out_specs=out_specs, check_vma=False
    )
```

```python
import functools

import jax
import jax.numpy as jnp
from jax import lax
from jax.experimental import pallas as pl
from jax.experimental.pallas import tpu as pltpu
from jax.sharding import PartitionSpec as P

MESH = pl.DeviceIdType.MESH
VMEM = pltpu.VMEM
F32 = jnp.float32
BF16 = jnp.bfloat16
LANES = 128


def vmem_specs(count):
    return [pl.BlockSpec(memory_space=pltpu.VMEM)] * count


def greet(groups):
    barrier = pltpu.get_barrier_semaphore()
    total = 0
    for axis, size in groups:
        me = lax.axis_index(axis)
        for step in range(1, size):
            peer = lax.rem(me + step, size)
            pl.semaphore_signal(barrier, inc=1, device_id={axis: peer}, device_id_type=MESH)
            total += 1
    pl.semaphore_wait(barrier, total)


def lane_of(shape):
    return lax.broadcasted_iota(jnp.int32, shape, len(shape) - 1)


def roll(x, shift):
    return pltpu.roll(x, shift % LANES, x.ndim - 1)


def score_kernel(
    dims, place_ref, w_ref, r_ref, t_ref, sigma_ref, parts, weights_ref, tall, wall, rall, rows_ref,
    table, low, high, pick_num, pick_den,
    own_sem, ws, wr, rs, rr, ts, tr, ls, lr,
):
    fellows, particles, owners, per_owner, slots, top, angles, half = dims
    width = 2 * half
    per_pack = LANES // width
    per_den = LANES // half
    tall_rows = table.shape[1]
    num_packs = particles // per_pack
    tiles = angles // 8
    cut = (tiles // 2 + tiles % 2) * 8
    my_owner = lax.axis_index("cls")
    my_fellow = lax.axis_index("img")
    greet((("cls", owners), ("img", fellows)))

    def remote(src, dst, send, recv, axis, peer):
        return pltpu.make_async_remote_copy(
            src_ref=src,
            dst_ref=dst,
            send_sem=send,
            recv_sem=recv,
            device_id={axis: peer},
            device_id_type=MESH,
        )

    row_copies = []
    ref_copies = []
    image_copies = []
    for step in range(1, fellows):
        peer = lax.rem(my_fellow + step, fellows)
        row_copies.append(remote(t_ref, tall.at[my_fellow], ts.at[step], tr.at[step], "img", peer))
        image_copies.append(
            remote(w_ref.at[peer], wall.at[my_fellow], ws.at[step], wr.at[step], "img", peer)
        )
    for step in range(1, owners):
        peer = lax.rem(my_owner + step, owners)
        ref_copies.append(remote(r_ref, rall.at[my_owner], rs.at[step], rr.at[step], "cls", peer))
    for copy in row_copies + ref_copies + image_copies:
        copy.start()
    own_rows = pltpu.make_async_copy(t_ref, tall.at[my_fellow], own_sem.at[0])
    own_rows.start()

    lane = lane_of((angles, LANES))
    zero_tail = jnp.zeros((LANES - angles, LANES), F32)
    source_lane = lax.broadcasted_iota(jnp.int32, (LANES, LANES), 0)
    target_lane = lax.broadcasted_iota(jnp.int32, (LANES, LANES), 1)
    shell = target_lane % half
    num_source = jnp.where(target_lane < width, 2 * shell + target_lane // half, -LANES)
    for g in range(per_pack):
        pick_num[g] = (source_lane == num_source + width * g).astype(F32).astype(BF16)
    den_source = jnp.where(target_lane < width + half, shell, -LANES)
    for g in range(per_den):
        pick_den[g] = (source_lane == den_source + half * g).astype(F32).astype(BF16)
    spread = jnp.concatenate([1.0 / sigma_ref[...]] * (LANES // sigma_ref.shape[1]), axis=1)
    spread = jnp.broadcast_to(spread, (8, LANES))
    row_lane = lane_of((8, LANES))
    inverse = jnp.zeros((8, LANES), F32)
    for part in range(3):
        shift = lax.rem(half * part - half * my_fellow + LANES, LANES)
        inverse = jnp.where(row_lane // half == part, pltpu.roll(spread, shift, 1), inverse)
    inverse = inverse[0:1]

    def place(fellow, read):
        def some(u, carry):
            for g in range(per_den):
                num = jnp.dot(
                    read(u * (per_den // per_pack) + g // per_pack),
                    pick_num[g % per_pack],
                    preferred_element_type=F32,
                )
                den = jnp.dot(read(num_packs + u), pick_den[g], preferred_element_type=F32)
                joined = jnp.where(lane < width, num, den) * (den * inverse)
                weights_ref[fellow * particles + u * per_den + g] = jnp.concatenate(
                    [joined, zero_tail], axis=0
                ).astype(BF16)
            return carry

        lax.fori_loop(0, particles // per_den, some, 0)

    def tabulate(owner, read):
        for t in range(per_owner):
            ref = jnp.dot(read(t // per_pack), pick_num[t % per_pack], preferred_element_type=F32)
            square = ref * ref
            power = (square + roll(square, -half)).astype(BF16).astype(F32) * -0.5
            power = roll(power, width)
            joined = jnp.where(lane < width, ref, jnp.where(lane < width + half, power, 0.0))
            table[owner * per_owner + t] = jnp.concatenate(
                [joined, jnp.zeros((tall_rows - angles, LANES), F32)], axis=0
            ).astype(BF16)

    tabulate(my_owner, lambda u: r_ref[u])
    place(my_fellow, lambda u: w_ref[my_fellow, u])
    own_rows.wait()
    for copy in row_copies:
        copy.wait_recv()
    to_smem = pltpu.make_async_copy(tall, rows_ref, own_sem.at[1])
    to_smem.start()
    for step in range(1, owners):
        ref_copies[step - 1].wait_recv()
        holder = lax.rem(my_owner + owners - step, owners)
        tabulate(holder, lambda u: rall[holder, u])
    to_smem.wait()

    batch = 8

    def score(fellow, begin):
        lows = []
        highs = []
        for k in range(batch):
            i = begin + k
            refs = jnp.concatenate([table[place_ref[rows_ref[fellow, i, j]]] for j in range(top)], axis=0)
            grid = lax.dot_general(
                refs,
                weights_ref[fellow * particles + i],
                (((1,), (1,)), ((), ())),
                preferred_element_type=F32,
            )
            for j in range(top):
                base = j * tall_rows
                lo = grid[base : base + 8]
                for tile in range(1, cut // 8):
                    lo = lo + roll(grid[base + 8 * tile : base + 8 * tile + 8], 8 * tile)
                hi = grid[base + cut : base + cut + 8]
                for tile in range(cut // 8 + 1, tiles):
                    hi = hi + roll(grid[base + 8 * tile : base + 8 * tile + 8], 8 * tile - cut)
                lo = pltpu.roll(lo, 0, 1, stride=1, stride_axis=0)
                hi = pltpu.roll(hi, 0, 1, stride=1, stride_axis=0)
                lows.append(jnp.sum(lo, axis=0, keepdims=True))
                highs.append(jnp.sum(hi, axis=0, keepdims=True))
        rows = batch * top
        start = pl.multiple_of(begin * top, rows)
        low[pl.ds(start, rows)] = jnp.concatenate(lows, axis=0)
        high[pl.ds(start, rows)] = jnp.concatenate(highs, axis=0)

    part_copies = []
    chunk = particles * top
    for turn in range(fellows):
        fellow = lax.rem(my_fellow + fellows - turn, fellows)
        if turn:
            image_copies[turn - 1].wait_recv()
            place(fellow, lambda u: wall[fellow, u])

        def some(b, carry):
            score(fellow, b * batch)
            return carry

        lax.fori_loop(0, particles // batch, some, 0)
        lo = low[...]
        hi = high[...]
        spot = lane_of(lo.shape)
        total = roll(lo, 1) + jnp.where(spot < cut, roll(lo, 1 - angles), 0.0)
        back = angles - 1 - cut
        total = total + roll(hi, -back) + jnp.where(spot >= cut + 1, roll(hi, cut + 1), 0.0)
        begin = pl.multiple_of(fellow * chunk, chunk)
        place_at = parts.at[my_fellow, pl.ds(begin, chunk)]
        parts[my_fellow, pl.ds(begin, chunk)] = jnp.where(spot < angles, total, 0.0)
        for step in range(1, fellows):
            peer = lax.rem(my_fellow + step, fellows)
            copy = remote(place_at, place_at, ls.at[step, turn], lr.at[step, turn], "img", peer)
            copy.start()
            part_copies.append(copy)
    for copy in row_copies + ref_copies + image_copies:
        copy.wait_send()
    for copy in part_copies:
        copy.wait()


def group_of(x, top, combine):
    row = lax.broadcasted_iota(jnp.int32, x.shape, 0)
    count = x.shape[0]
    step = 1
    while step < top:
        swapped = jnp.where(
            (row // step) % 2 == 0, pltpu.roll(x, count - step, 0), pltpu.roll(x, step, 0)
        )
        x = combine(x, swapped)
        step *= 2
    return x


def total_kernel(dims, place_ref, rows_ref, parts, weights_ref, out_ref, acc, ext_lo, ext_hi):
    fellows, particles, owners, per_owner, slots, top, angles, half = dims
    width = 2 * half
    per_pack = LANES // width
    per_den = LANES // half
    num_packs = slots // per_pack
    cut = (angles // 16) * 8 + (8 if (angles // 8) % 2 else 0)
    tiles = angles // 8
    tall_rows = -(-angles // 16) * 16
    logits = parts[0]
    for fellow in range(1, fellows):
        logits = logits + parts[fellow]
    spot = lane_of(logits.shape)
    inside = spot < angles
    highest = jnp.max(jnp.where(inside, logits, -jnp.inf), axis=1, keepdims=True)
    highest = group_of(jnp.broadcast_to(highest, logits.shape), top, jnp.maximum)
    exponent = jnp.where(inside, jnp.exp(logits - highest), 0.0)
    summed = jnp.sum(exponent, axis=1, keepdims=True)
    summed = group_of(jnp.broadcast_to(summed, logits.shape), top, jnp.add)
    post = (exponent / summed).astype(BF16).astype(F32)
    lo = jnp.where(inside, post, roll(post, LANES - angles))
    hi = jnp.where((spot >= cut) & inside, roll(post, cut), roll(post, cut - angles))
    ext_lo[...] = lo.reshape(ext_lo.shape)
    ext_hi[...] = hi.reshape(ext_hi.shape)
    acc[...] = jnp.zeros_like(acc)

    def pair(m):
        lo_rows = ext_lo[m]
        hi_rows = ext_hi[m]
        for k in range(2):
            i = 2 * m + k
            turned = []
            for j in range(top):
                e = k * top + j
                first = pltpu.roll(
                    jnp.broadcast_to(lo_rows[e : e + 1], (8, LANES)), 0, 1, stride=1, stride_axis=0
                )
                second = pltpu.roll(
                    jnp.broadcast_to(hi_rows[e : e + 1], (8, LANES)), 0, 1, stride=1, stride_axis=0
                )
                for tile in range(tiles):
                    if 8 * tile < cut:
                        turned.append(roll(first, 8 * tile) if tile else first)
                    else:
                        shift = 8 * tile - cut
                        turned.append(roll(second, shift) if shift else second)
                for tile in range(tiles, tall_rows // 8):
                    turned.append(second)
            circle = jnp.concatenate(turned, axis=0).astype(BF16)
            grid = jnp.dot(circle, weights_ref[i], preferred_element_type=F32)
            spots = [place_ref[rows_ref[i, j]] for j in range(top)]
            held = [acc[spot] for spot in spots]
            for j in range(top):
                acc[spots[j]] = held[j] + grid[j * tall_rows : j * tall_rows + angles]

    def some(b, carry):
        for m in range(batch // 2):
            pair(b * (batch // 2) + m)
        return carry

    batch = 8
    lax.fori_loop(0, ext_lo.shape[0] // (batch // 2), some, 0)
    lane = lane_of((angles, LANES))

    def pack(owner, carry):
        nums = [None] * num_packs
        dens = [None] * -(-slots // per_den)
        for t in range(per_owner):
            value = acc[owner * per_owner + t]
            g, u = t % per_pack, t // per_pack
            num = roll(value, width * g)
            nums[u] = num if g == 0 else jnp.where(lane >= width * g, num, nums[u])
            h, v = t % per_den, t // per_den
            den = roll(value, half * h - width)
            dens[v] = den if h == 0 else jnp.where(lane >= half * h, den, dens[v])
        for u, value in enumerate(nums + dens):
            out_ref[owner, u] = value.astype(BF16)
        return carry

    lax.fori_loop(0, owners, pack, 0)


def gather_kernel(axis, size, half, slots, x_ref, out_ref, landed, send, recv):
    me = lax.axis_index(axis)
    greet(((axis, size),))
    copies = []
    for step in range(1, size):
        peer = lax.rem(me + step, size)
        copies.append(
            pltpu.make_async_remote_copy(
                src_ref=x_ref.at[peer],
                dst_ref=landed.at[step - 1],
                send_sem=send.at[step],
                recv_sem=recv.at[step],
                device_id={axis: peer},
                device_id_type=MESH,
            )
        )
    for copy in copies:
        copy.start()
    total = x_ref[me].astype(F32)
    for step in range(1, size):
        copies[step - 1].wait_recv()
        total = total + landed[step - 1].astype(F32)
    width = 2 * half
    per_pack = LANES // width
    num_packs = slots // per_pack
    target = lax.broadcasted_iota(jnp.int32, (LANES, LANES), 0)
    source = lax.broadcasted_iota(jnp.int32, (LANES, LANES), 1)
    shell = (target % width) // 2
    flip = target - target % width + (target % 2) * half + shell

    def picked(wanted, x):
        return lax.dot_general(
            (source == wanted).astype(F32),
            x,
            (((1,), (1,)), ((), ())),
            precision=lax.Precision.HIGHEST,
            preferred_element_type=F32,
        )

    for u in range(num_packs):
        held = num_packs + (u * per_pack * half) // LANES
        offset = (u * per_pack * half) % LANES
        den = picked(offset + half * (target // width) + shell, total[held])
        out_ref[u] = picked(flip, total[u]) / (den + 1.0)
    for copy in copies:
        copy.wait_send()


def on_device(images, ctf, classes, class_place, references, sigma2):
    shells = sigma2.shape[0]
    angles = ctf.shape[1] // shells
    particles = images.shape[0]
    per_owner = references.shape[0]
    top = classes.shape[1]
    owners = lax.axis_size("cls")
    fellows = lax.axis_size("img")
    my_fellow = lax.axis_index("img")
    half = shells // fellows
    width = 2 * half
    per_pack = LANES // width
    per_den = LANES // half
    slots = -(-per_owner // per_pack) * per_pack
    dims = (fellows, particles, owners, per_owner, slots, top, angles, half)

    num = images.reshape(particles // per_pack, per_pack, fellows, width, angles)
    num = num.transpose(2, 0, 4, 1, 3).reshape(fellows, -1, angles, LANES)
    den = ctf.reshape(particles // per_den, per_den, fellows, half, angles)
    den = den.transpose(2, 0, 4, 1, 3).reshape(fellows, -1, angles, LANES)
    send = jnp.concatenate([num, den], axis=1)
    mine = lax.dynamic_slice_in_dim(references, my_fellow * (width * angles), width * angles, 1)
    mine = jnp.pad(mine, ((0, slots - per_owner), (0, 0)))
    mine = mine.reshape(slots // per_pack, per_pack, width, angles)[..., ::-1]
    mine = mine.transpose(0, 3, 1, 2).reshape(-1, angles, LANES)
    rows = jnp.pad(classes, ((0, 0), (0, LANES - top)))

    packs = send.shape[1]
    everyone = fellows * particles
    tall_rows = -(-angles // 16) * 16
    pairs = everyone // 2
    smem = pl.BlockSpec(memory_space=pltpu.SMEM)
    dma = pltpu.SemaphoreType.DMA
    parts, weights, tall = pl.pallas_call(
        functools.partial(score_kernel, dims),
        out_shape=(
            jax.ShapeDtypeStruct((fellows, everyone * top, LANES), F32),
            jax.ShapeDtypeStruct((everyone, LANES, LANES), BF16),
            jax.ShapeDtypeStruct((fellows, particles, LANES), jnp.int32),
        ),
        in_specs=[smem] + vmem_specs(4),
        out_specs=tuple(vmem_specs(3)),
        scratch_shapes=[
            VMEM((fellows, packs, angles, LANES), BF16),
            VMEM((owners,) + mine.shape, BF16),
            pltpu.SMEM((fellows, particles, LANES), jnp.int32),
            VMEM((owners * per_owner, tall_rows, LANES), BF16),
            VMEM((particles * top, LANES), F32),
            VMEM((particles * top, LANES), F32),
            VMEM((per_pack, LANES, LANES), BF16),
            VMEM((per_den, LANES, LANES), BF16),
            dma((2,)),
            dma((fellows,)),
            dma((fellows,)),
            dma((owners,)),
            dma((owners,)),
            dma((fellows,)),
            dma((fellows,)),
            dma((fellows, fellows)),
            dma((fellows, fellows)),
        ],
        compiler_params=pltpu.CompilerParams(collective_id=0, has_side_effects=True),
    )(class_place, send, mine, rows, sigma2.reshape(1, shells))
    row_list = tall[:, :, :top].reshape(everyone, top)
    sums = pl.pallas_call(
        functools.partial(total_kernel, dims),
        out_shape=jax.ShapeDtypeStruct(
            (owners, slots // per_pack - (-slots // per_den), angles, LANES), BF16
        ),
        in_specs=[smem, smem] + vmem_specs(2),
        out_specs=pl.BlockSpec(memory_space=pltpu.VMEM),
        scratch_shapes=[
            VMEM((owners * per_owner, angles, LANES), F32),
            VMEM((pairs, 2 * top, LANES), F32),
            VMEM((pairs, 2 * top, LANES), F32),
        ],
    )(class_place, row_list, parts, weights)
    share = pl.pallas_call(
        functools.partial(gather_kernel, "cls", owners, half, slots),
        out_shape=jax.ShapeDtypeStruct((slots // per_pack, LANES, angles), F32),
        in_specs=vmem_specs(1),
        out_specs=pl.BlockSpec(memory_space=pltpu.VMEM),
        scratch_shapes=[
            VMEM((owners - 1,) + sums.shape[1:], BF16),
            pltpu.SemaphoreType.DMA((owners,)),
            pltpu.SemaphoreType.DMA((owners,)),
        ],
        compiler_params=pltpu.CompilerParams(collective_id=2, has_side_effects=True),
    )(sums)
    return share.reshape(slots * width, angles)[: per_owner * width].reshape(per_owner, -1)


def solution(mesh):
    in_specs = (
        P(("cls", "img"), None),
        P(("cls", "img"), None),
        P(("cls", "img"), None),
        P(),
        P("cls", None),
        P(),
    )
    out_specs = P("cls", "img")
    return jax.shard_map(
        on_device, mesh=mesh, in_specs=in_specs, out_specs=out_specs, check_vma=False
    )
```
